32 devices in a mesh: dp: 4 (over y, x), section: 2 (over core), tensor: 4 (over z).
Axes of the slice: x: 2, y: 2, z: 4, core: 2. Of those that a mesh axis runs over, the one named last changes fastest.
Arguments:
- stored: bfloat16 [2, 2, 256, 8192], P('section', None, 'dp', 'tensor'), may hold values from -6 to 6
- cotangent: bfloat16 [2, 32, 8192], P(None, None, 'tensor'), may hold values from -12 to 12
- positions: int32 [2, 32], replicated, may hold values from 128 to 255, as said below
- lengths: int32 [2], replicated, may hold values from 128 to 256, as said below
- norm_gain: float32 [2, 8192], P('section'), may hold values from 0.5 to 1.5
- w_query: bfloat16 [2, 8192, 8192], P('section', None, 'tensor')
- w_key: bfloat16 [2, 8192, 1024], P('section', None, 'tensor')
- w_value: bfloat16 [2, 8192, 1024], P('section', None, 'tensor'), may hold values from -0.0625 to 0.0625
- w_out: bfloat16 [2, 8192, 8192], P('section', 'tensor', 'dp'), may hold values from -0.0625 to 0.0625
Outputs:
- input_grads: float32 [2, 2, 256, 8192], P('section', None, 'dp', 'tensor')
The draws below stay inside these ranges and needn't reach their ends.
Inputs may be any that keep to these rules, and one draw needn't show every extreme that they name: In each sequence the response positions are distinct, rise along the last dimension, lie in the last 128 positions, and the last one is 255. `lengths`: some sequence has length 256.
All inputs are finite; a program needn't handle non-finite values.
Results may differ from the reference program's by a relative error of at most 0.017.
Values may be sent and summed in bfloat16 or wider, within the bound.
A program may use at most 256 MiB of HBM per device.

```python
import math
import jax
import jax.numpy as jnp
from jax import lax

D = 8192
HEADS = 64
KV = 8
HD = 128
RESP = 32
SEQS = 2
SEQ = 256
N_TENSOR = 4


def key_base(key):
    return jax.random.normal(jax.random.fold_in(key, 101), (2, D, KV * HD), jnp.float32) / math.sqrt(D)


def draw_w_key(key, part):
    base = key_base(key)
    return base.astype(jnp.bfloat16)


def draw_w_query(key, part):
    noise = jax.random.normal(jax.random.fold_in(key, 202), (2, D, HEADS * HD), jnp.float32) / math.sqrt(D)
    return noise.astype(jnp.bfloat16)


def length_draw(key):
    drawn = jax.random.randint(jax.random.fold_in(key, 404), (SEQS,), SEQ // 2, SEQ + 1)
    longest = jax.random.randint(jax.random.fold_in(key, 405), (), 0, SEQS)
    return jnp.where(jnp.arange(SEQS) == longest, SEQ, drawn).astype(jnp.int32)


def draw_lengths(key, part):
    return length_draw(key)


def draw_positions(key, part):
    span = 4 * RESP
    seq_keys = jax.random.split(jax.random.fold_in(key, 406), SEQS)
    picks = jax.vmap(lambda one_key: jnp.sort(jax.random.permutation(one_key, span - 1)[:RESP - 1]))(seq_keys)
    offsets = jnp.concatenate([picks, jnp.full((SEQS, 1), span - 1, jnp.int32)], 1)
    return (SEQ - span + offsets).astype(jnp.int32)


def block_levels(stream_key, shape, pieces, low, high):
    def one(axis_at, parts):
        heights = jax.random.uniform(jax.random.fold_in(jax.random.fold_in(stream_key, 6), axis_at), (parts,), jnp.float32, low / len(pieces), high / len(pieces))
        return jnp.repeat(jnp.exp(heights), shape[axis_at] // parts).reshape((-1,) + (1,) * (len(shape) - axis_at - 1))

    level = one(*pieces[0])
    for cut in pieces[1:]:
        level = level * one(*cut)
    return level


def scatter_about(key, dims, width, most, cuts=(), kind=jnp.bfloat16):
    entries = width * jax.random.normal(key, dims, jnp.float32)
    if cuts:
        entries = entries * block_levels(key, dims, cuts, -0.22, 0.18)
    return jnp.clip(entries, -most, most).astype(kind)


def setup_inputs(seed: int = 0) -> dict:
    seeds = jax.random.split(jax.random.key(seed), 10)
    return {
        "stored": scatter_about(seeds[0], (2, SEQS, SEQ, D), 1.0, 6.0, ((0, 2), (2, 4), (3, 4))),
        "cotangent": scatter_about(seeds[1], (SEQS, RESP, D), 2.0, 12.0, ((2, 4),)),
        "positions": draw_positions(jax.random.fold_in(seeds[9], 71), 0),
        "lengths": draw_lengths(jax.random.fold_in(seeds[9], 71), 0),
        "norm_gain": jnp.clip(1.0 + 0.1 * jax.random.normal(seeds[4], (2, D), jnp.float32), 0.5, 1.5),
        "w_query": draw_w_query(jax.random.fold_in(seeds[9], 71), 0),
        "w_key": draw_w_key(jax.random.fold_in(seeds[9], 71), 0),
        "w_value": scatter_about(seeds[7], (2, D, KV * HD), D ** -0.5, 0.0625, ((0, 2), (2, 4))),
        "w_out": scatter_about(seeds[8], (2, HEADS * HD, D), (HEADS * HD) ** -0.5, 0.0625, ((0, 2), (1, 4), (2, 4))),
    }


EPS = 1e-05
THETA = 500000.0

def angle_tables(count):
    half_dim = HD // 2
    frequency = THETA ** (-(jnp.arange(half_dim, dtype=jnp.float32) * 2.0) / HD)
    angles = jnp.arange(count, dtype=jnp.float32)[:, None] * frequency[None, :]
    cosine = jnp.concatenate([jnp.cos(angles), jnp.cos(angles)], -1)[:, None, :]
    sine_table = jnp.concatenate([jnp.sin(angles), jnp.sin(angles)], -1)[:, None, :]
    return (cosine, sine_table)

def turn_half(values):
    half_dim = values.shape[-1] // 2
    return jnp.concatenate([-values[..., half_dim:], values[..., :half_dim]], -1)

def rotate(values, cosine, sine_table):
    return values * cosine + turn_half(values) * sine_table

def unrotate(values, cosine, sine_table):
    return values * cosine - turn_half(values * sine_table)

def layer_grad(inputs, upstream, lengths, gain, w_query, w_key, w_value, w_out):
    q_cols = HEADS * HD // N_TENSOR
    kv_cols = KV * HD // N_TENSOR
    kv_dev = KV // N_TENSOR
    group = HEADS // KV
    scale = 1.0 / HD ** 0.5
    cosine, sine_table = angle_tables(SEQ)
    seq_ids = jnp.arange(SEQ, dtype=jnp.int32)

    def one_seq(packed):
        inputs_s, upstream_s, length_s = packed
        x_full = inputs_s.astype(jnp.float32)
        inv_rms = lax.rsqrt(lax.optimization_barrier(jnp.mean(x_full * x_full, -1, keepdims=True)) + EPS)
        normed = (x_full * inv_rms * gain).astype(jnp.bfloat16)
        start_pos = SEQ - length_s
        causal = seq_ids[None, :] <= seq_ids[:, None]
        valid = (seq_ids[None, :] >= start_pos) | (seq_ids[None, :] == seq_ids[:, None])
        allowed = causal & valid
        summed = jnp.zeros((SEQ, D), jnp.float32)
        for part in range(N_TENSOR):
            wq_part = w_query[:, part * q_cols:(part + 1) * q_cols]
            wk_part = w_key[:, part * kv_cols:(part + 1) * kv_cols]
            wv_part = w_value[:, part * kv_cols:(part + 1) * kv_cols]
            wo_part = w_out[part * q_cols:(part + 1) * q_cols, :]
            queries = jnp.dot(normed, wq_part, preferred_element_type=jnp.float32).reshape(SEQ, q_cols // HD, HD)
            keys = jnp.dot(normed, wk_part, preferred_element_type=jnp.float32).reshape(SEQ, kv_dev, HD)
            values = jnp.dot(normed, wv_part, preferred_element_type=jnp.float32).reshape(SEQ, kv_dev, HD)
            q_rot = rotate(queries, cosine, sine_table).astype(jnp.bfloat16)
            k_rot = rotate(keys, cosine, sine_table).astype(jnp.bfloat16).astype(jnp.float32)
            values_b = values.astype(jnp.bfloat16).astype(jnp.float32)
            grad_out = jnp.dot(upstream_s, wo_part.T, preferred_element_type=jnp.float32).astype(jnp.bfloat16)
            q_five = q_rot.reshape(SEQ, kv_dev, group, HD).astype(jnp.float32)
            o_five = grad_out.reshape(SEQ, kv_dev, group, HD).astype(jnp.float32)
            scores = jnp.einsum('pkgd,jkd->kgpj', q_five, k_rot) * scale
            masked = jnp.where(allowed, scores, -1e+30)
            highest = lax.optimization_barrier(jnp.max(masked, -1, keepdims=True))
            expo_terms = jnp.where(allowed, jnp.exp(masked - highest), 0.0)
            probs = expo_terms / lax.optimization_barrier(jnp.sum(expo_terms, -1, keepdims=True))
            grad_probs = jnp.einsum('pkgd,jkd->kgpj', o_five, values_b)
            row_dot = lax.optimization_barrier(jnp.sum(probs * grad_probs, -1, keepdims=True))
            grad_scores = (probs * (grad_probs - row_dot) * scale).astype(jnp.bfloat16).astype(jnp.float32)
            probs_b = probs.astype(jnp.bfloat16).astype(jnp.float32)
            grad_qr = jnp.einsum('kgpj,jkd->pkgd', grad_scores, k_rot).reshape(SEQ, q_cols // HD, HD)
            grad_kr = jnp.einsum('kgpj,pkgd->jkd', grad_scores, q_five)
            grad_vr = jnp.einsum('kgpj,pkgd->jkd', probs_b, o_five)
            grad_q = unrotate(grad_qr, cosine, sine_table).astype(jnp.bfloat16).reshape(SEQ, q_cols)
            grad_k = unrotate(grad_kr, cosine, sine_table).astype(jnp.bfloat16).reshape(SEQ, kv_cols)
            grad_v = grad_vr.astype(jnp.bfloat16).reshape(SEQ, kv_cols)
            partial_term = jnp.dot(grad_q, wq_part.T, preferred_element_type=jnp.float32)
            partial_term = partial_term + jnp.dot(grad_k, wk_part.T, preferred_element_type=jnp.float32)
            partial_term = partial_term + jnp.dot(grad_v, wv_part.T, preferred_element_type=jnp.float32)
            summed = summed + lax.optimization_barrier(partial_term.astype(jnp.bfloat16)).astype(jnp.float32)
        stat = lax.optimization_barrier(jnp.sum(x_full * gain * summed, -1, keepdims=True))
        return upstream_s.astype(jnp.float32) + inv_rms * gain * summed - x_full * inv_rms ** 3 * stat / D
    return lax.map(one_seq, (inputs, upstream, lengths))

def reference(stored, cotangent, positions, lengths, norm_gain, w_query, w_key, w_value, w_out):
    seq_ids = jnp.arange(SEQ, dtype=jnp.int32)
    hits = (positions[:, :, None] == seq_ids[None, None, :]).astype(jnp.float32)
    from_loss = jnp.einsum('srp,srd->spd', hits, cotangent.astype(jnp.float32)).astype(jnp.bfloat16)
    upper = layer_grad(stored[1], from_loss, lengths, norm_gain[1], w_query[1], w_key[1], w_value[1], w_out[1])
    lower = layer_grad(stored[0], upper.astype(jnp.bfloat16), lengths, norm_gain[0], w_query[0], w_key[0], w_value[0], w_out[0])
    return jnp.stack([lower, upper])
```

```python
import functools
import math

import jax
import jax.numpy as jnp
from jax import lax
from jax.experimental import pallas as pl
from jax.experimental.pallas import tpu as pltpu
from jax.sharding import PartitionSpec as P

HD = 128
EPS = 1e-05
THETA = 500000.0
F32 = jnp.float32
BF16 = jnp.bfloat16


def dot_t(left, right):
    return lax.dot_general(left, right, (((1,), (1,)), ((), ())), preferred_element_type=F32)


def dot_n(left, right):
    return lax.dot_general(left, right, (((1,), (0,)), ((), ())), preferred_element_type=F32)


def dot_c(left, right):
    return lax.dot_general(left, right, (((0,), (0,)), ((), ())), preferred_element_type=F32)


def angle_tables(row_places):
    half_dim = HD // 2
    frequency = THETA ** (-(jnp.arange(half_dim, dtype=F32) * 2.0) / HD)
    angles = row_places[:, None] * frequency[None, :]
    cosine = jnp.concatenate([jnp.cos(angles), jnp.cos(angles)], -1)
    signed_sine = jnp.concatenate([-jnp.sin(angles), jnp.sin(angles)], -1)
    return cosine, signed_sine


def turn_plain(values):
    half_dim = HD // 2
    return jnp.concatenate([values[..., half_dim:], values[..., :half_dim]], -1)


def attention_body(lens_ref, q_ref, o_ref, k_ref, v_ref, cos_ref, sin_ref, gq_ref, gk_ref, gv_ref):
    seq = pl.program_id(0)
    rows = q_ref.shape[1]
    length = k_ref.shape[1]
    group = q_ref.shape[2] // HD
    scale = 1.0 / math.sqrt(HD)
    cosine, sine = cos_ref[...], sin_ref[...]
    q_parts, o_parts = [], []
    for head in range(group):
        lanes = slice(head * HD, (head + 1) * HD)
        raw = q_ref[0, :, lanes]
        q_parts.append((raw * cosine + pltpu.roll(raw, HD // 2, 1) * sine).astype(BF16))
        o_parts.append(o_ref[0, :, lanes])
    q_all = jnp.concatenate(q_parts, 0)
    o_all = jnp.concatenate(o_parts, 0)
    keys, values = k_ref[0], v_ref[0]
    many = rows * group
    row_at = lax.broadcasted_iota(jnp.int32, (many, length), 0) & (rows - 1)
    query_at = lens_ref[1, 0] + row_at
    key_at = lax.broadcasted_iota(jnp.int32, (many, length), 1)
    start = length - lens_ref[0, seq]
    allowed = (key_at == query_at) | ((key_at < query_at) & (key_at >= start))
    scores = jnp.where(allowed, dot_t(q_all, keys) * scale, -1e30)
    highest = jnp.max(scores, -1, keepdims=True)
    terms = jnp.where(allowed, jnp.exp(scores - highest), 0.0)
    probs = terms / jnp.sum(terms, -1, keepdims=True)
    grad_probs = dot_t(o_all, values)
    row_dot = jnp.sum(probs * grad_probs, -1, keepdims=True)
    grad_scores = (probs * (grad_probs - row_dot) * scale).astype(BF16)
    grad_qr = dot_n(grad_scores, keys)
    gk_ref[0] = dot_c(grad_scores, q_all).astype(BF16)
    gv_ref[0] = dot_c(probs.astype(BF16), o_all).astype(BF16)
    for head in range(group):
        part = grad_qr[head * rows : (head + 1) * rows]
        turned = part * cosine - pltpu.roll(part, HD // 2, 1) * sine
        gq_ref[0, :, head * HD : (head + 1) * HD] = turned.astype(BF16)


def attention_grad(lens, queries, grad_out, keys, values, cosine, sine):
    batch, rows, cols = queries.shape
    length = keys.shape[1]
    kv_dev = keys.shape[2] // HD
    group_cols = cols // kv_dev
    q_spec = pl.BlockSpec((1, rows, group_cols), lambda b, h: (b, 0, h))
    k_spec = pl.BlockSpec((1, length, HD), lambda b, h: (b, 0, h))
    t_spec = pl.BlockSpec((rows, HD), lambda b, h: (0, 0))
    return pl.pallas_call(
        attention_body,
        grid=(batch, kv_dev),
        in_specs=[
            pl.BlockSpec(memory_space=pltpu.SMEM),
            q_spec,
            q_spec,
            k_spec,
            k_spec,
            t_spec,
            t_spec,
        ],
        out_specs=[q_spec, k_spec, k_spec],
        out_shape=[
            jax.ShapeDtypeStruct((batch, rows, cols), BF16),
            jax.ShapeDtypeStruct((batch, length, kv_dev * HD), BF16),
            jax.ShapeDtypeStruct((batch, length, kv_dev * HD), BF16),
        ],
        compiler_params=pltpu.CompilerParams(vmem_limit_bytes=32 * 1024 * 1024),
    )(lens, queries, grad_out, keys, values, cosine, sine)


def on_device(
    n_dp, n_tensor, stored, cotangent, positions, lengths, norm_gain, w_query, w_key, w_value, w_out
):
    x_own = stored[0]
    gain = norm_gain[0]
    w_q, w_k, w_v, w_o = w_query[0], w_key[0], w_value[0], w_out[0]
    seqs, rows, width_dev = x_own.shape
    many = seqs * rows
    width = gain.shape[0]
    kv_cols = w_k.shape[1]
    dp_id = lax.axis_index("dp")
    tensor_id = lax.axis_index("tensor")
    section_id = lax.axis_index("section")
    swap = [(d * n_tensor + t, t * n_tensor + d) for d in range(n_dp) for t in range(n_tensor)]

    row_ids = dp_id * rows + jnp.arange(rows, dtype=jnp.int32)
    cosine, sine = angle_tables(row_ids.astype(F32))
    lens = jnp.stack(
        [lengths, jnp.full_like(lengths, dp_id * rows)], 0
    )

    cot_slice = lax.ppermute(cotangent, ("dp", "tensor"), swap)
    resp = cotangent.shape[1]
    resp_part = dot_t(cot_slice.reshape(seqs * resp, width_dev), w_o)
    resp_grad = lax.psum(resp_part.astype(BF16), "dp").reshape(seqs, resp, -1)
    placed = (positions[:, None, :] == row_ids[None, :, None]).astype(BF16)

    def place(small):
        return jnp.einsum("spr,srd->spd", placed, small, preferred_element_type=F32).astype(BF16)

    x_whole = lax.all_gather(x_own, "tensor", axis=2, tiled=True)
    x_full = x_whole.astype(F32)
    inv_rms = lax.rsqrt(jnp.mean(x_full * x_full, -1, keepdims=True) + EPS)
    normed = (x_full * inv_rms * gain).astype(BF16).reshape(many, width)
    queries, keys, values = lax.optimization_barrier(
        (dot_n(normed, w_q), dot_n(normed, w_k), dot_n(normed, w_v))
    )
    k_four = keys.reshape(seqs, rows, -1, HD)
    k_rot = k_four * cosine[:, None] + turn_plain(k_four) * sine[:, None]
    kv_own = jnp.concatenate(
        [k_rot.reshape(seqs, rows, kv_cols), values.reshape(seqs, rows, kv_cols)], -1
    ).astype(BF16)
    kv_all = lax.all_gather(kv_own, "dp", axis=1, tiled=True)
    k_all, v_all = kv_all[..., :kv_cols], kv_all[..., kv_cols:]
    queries = queries.reshape(seqs, rows, -1)
    gain_own = lax.dynamic_slice_in_dim(gain, tensor_id * width_dev, width_dev, 0)
    x_mine = x_own.astype(F32)

    def backward(upstream_own, grad_out):
        grad_q, key_terms, value_terms = attention_grad(
            lens, queries, grad_out, k_all, v_all, cosine, sine
        )
        kv_sum = lax.psum_scatter(
            jnp.concatenate([key_terms, value_terms], -1), "dp", scatter_dimension=1, tiled=True
        ).astype(F32)
        gk_four = kv_sum[..., :kv_cols].reshape(seqs, rows, -1, HD)
        grad_k = gk_four * cosine[:, None] - turn_plain(gk_four) * sine[:, None]
        grad_k = grad_k.astype(BF16).reshape(many, kv_cols)
        grad_v = kv_sum[..., kv_cols:].astype(BF16).reshape(many, kv_cols)
        partial = dot_t(grad_q.reshape(many, -1), w_q) + dot_t(grad_k, w_k) + dot_t(grad_v, w_v)
        summed = lax.psum_scatter(
            partial.astype(BF16), "tensor", scatter_dimension=1, tiled=True
        ).astype(F32)
        summed = summed.reshape(seqs, rows, width_dev)
        stat = lax.psum(jnp.sum(x_mine * gain_own * summed, -1, keepdims=True), "tensor")
        return (
            upstream_own.astype(F32)
            + inv_rms * gain_own * summed
            - x_mine * inv_rms**3 * stat / width
        )

    first = backward(place(cotangent), place(resp_grad))

    first_b = first.astype(BF16)
    down = [(1, 0)]
    handed = lax.ppermute(first_b, "section", down)
    across = [
        ((d * 2 + 1) * n_tensor + t, (t * 2) * n_tensor + d)
        for d in range(n_dp)
        for t in range(n_tensor)
    ]
    crossed = lax.ppermute(first_b, ("dp", "section", "tensor"), across)
    up_rows = lax.all_gather(crossed, "tensor", axis=0, tiled=False)
    up_part = dot_t(up_rows.reshape(n_dp * many, width_dev), w_o).astype(BF16)
    grad_out = lax.psum_scatter(up_part, "dp", scatter_dimension=0, tiled=True)
    second = backward(handed, grad_out.reshape(seqs, rows, -1))
    return jnp.where(section_id == 0, second, first)[None]


def solution(mesh):
    return jax.shard_map(
        functools.partial(on_device, mesh.shape["dp"], mesh.shape["tensor"]),
        mesh=mesh,
        in_specs=(
            P("section", None, "dp", "tensor"),
            P(None, None, "tensor"),
            P(),
            P(),
            P("section", None),
            P("section", None, "tensor"),
            P("section", None, "tensor"),
            P("section", None, "tensor"),
            P("section", "tensor", "dp"),
        ),
        out_specs=P("section", None, "dp", "tensor"),
        check_vma=False,
    )
```

```python
import functools
import math

import jax
import jax.numpy as jnp
from jax import lax
from jax.experimental import pallas as pl
from jax.experimental.pallas import tpu as pltpu
from jax.sharding import PartitionSpec as P

HD = 128
EPS = 1e-05
THETA = 500000.0
F32 = jnp.float32
BF16 = jnp.bfloat16


def dot_t(left, right):
    return lax.dot_general(left, right, (((1,), (1,)), ((), ())), preferred_element_type=F32)


def dot_n(left, right):
    return lax.dot_general(left, right, (((1,), (0,)), ((), ())), preferred_element_type=F32)


def dot_c(left, right):
    return lax.dot_general(left, right, (((0,), (0,)), ((), ())), preferred_element_type=F32)


def angle_tables(row_places):
    half_dim = HD // 2
    frequency = THETA ** (-(jnp.arange(half_dim, dtype=F32) * 2.0) / HD)
    angles = row_places[:, None] * frequency[None, :]
    cosine = jnp.concatenate([jnp.cos(angles), jnp.cos(angles)], -1)
    signed_sine = jnp.concatenate([-jnp.sin(angles), jnp.sin(angles)], -1)
    return cosine, signed_sine


def turn_plain(values):
    half_dim = HD // 2
    return jnp.concatenate([values[..., half_dim:], values[..., :half_dim]], -1)


def attention_body(lens_ref, q_ref, o_ref, k_ref, v_ref, cos_ref, sin_ref, gq_ref, gk_ref, gv_ref):
    seq = pl.program_id(0)
    rows = q_ref.shape[1]
    length = k_ref.shape[1]
    group = q_ref.shape[2] // HD
    scale = 1.0 / math.sqrt(HD)
    cosine, sine = cos_ref[...], sin_ref[...]
    q_parts, o_parts = [], []
    for head in range(group):
        lanes = slice(head * HD, (head + 1) * HD)
        raw = q_ref[0, :, lanes]
        q_parts.append((raw * cosine + pltpu.roll(raw, HD // 2, 1) * sine).astype(BF16))
        o_parts.append(o_ref[0, :, lanes])
    q_all = jnp.concatenate(q_parts, 0)
    o_all = jnp.concatenate(o_parts, 0)
    keys, values = k_ref[0], v_ref[0]
    many = rows * group
    row_at = lax.broadcasted_iota(jnp.int32, (many, length), 0) & (rows - 1)
    query_at = lens_ref[1, 0] + row_at
    key_at = lax.broadcasted_iota(jnp.int32, (many, length), 1)
    start = length - lens_ref[0, seq]
    allowed = (key_at == query_at) | ((key_at < query_at) & (key_at >= start))
    scores = jnp.where(allowed, dot_t(q_all, keys) * scale, -1e30)
    highest = jnp.max(scores, -1, keepdims=True)
    terms = jnp.where(allowed, jnp.exp(scores - highest), 0.0)
    probs = terms / jnp.sum(terms, -1, keepdims=True)
    grad_probs = dot_t(o_all, values)
    row_dot = jnp.sum(probs * grad_probs, -1, keepdims=True)
    grad_scores = (probs * (grad_probs - row_dot) * scale).astype(BF16)
    grad_qr = dot_n(grad_scores, keys)
    gk_ref[0] = dot_c(grad_scores, q_all).astype(BF16)
    gv_ref[0] = dot_c(probs.astype(BF16), o_all).astype(BF16)
    for head in range(group):
        part = grad_qr[head * rows : (head + 1) * rows]
        turned = part * cosine - pltpu.roll(part, HD // 2, 1) * sine
        gq_ref[0, :, head * HD : (head + 1) * HD] = turned.astype(BF16)


def attention_grad(lens, queries, grad_out, keys, values, cosine, sine):
    batch, rows, cols = queries.shape
    length = keys.shape[1]
    kv_dev = keys.shape[2] // HD
    group_cols = cols // kv_dev
    q_spec = pl.BlockSpec((1, rows, group_cols), lambda b, h: (b, 0, h))
    k_spec = pl.BlockSpec((1, length, HD), lambda b, h: (b, 0, h))
    t_spec = pl.BlockSpec((rows, HD), lambda b, h: (0, 0))
    return pl.pallas_call(
        attention_body,
        grid=(batch, kv_dev),
        in_specs=[
            pl.BlockSpec(memory_space=pltpu.SMEM),
            q_spec,
            q_spec,
            k_spec,
            k_spec,
            t_spec,
            t_spec,
        ],
        out_specs=[q_spec, k_spec, k_spec],
        out_shape=[
            jax.ShapeDtypeStruct((batch, rows, cols), BF16),
            jax.ShapeDtypeStruct((batch, length, kv_dev * HD), BF16),
            jax.ShapeDtypeStruct((batch, length, kv_dev * HD), BF16),
        ],
        compiler_params=pltpu.CompilerParams(vmem_limit_bytes=32 * 1024 * 1024),
    )(lens, queries, grad_out, keys, values, cosine, sine)


MESH = pl.DeviceIdType.MESH
BIG = 56 * 1024 * 1024


def at(dp, section, tensor):
    return {"dp": dp, "section": section, "tensor": tensor}


def greet(where):
    pl.semaphore_signal(
        pltpu.get_barrier_semaphore(), inc=1, device_id=where, device_id_type=MESH
    )


def remote(src, dst, send_sem, recv_sem, where):
    return pltpu.make_async_remote_copy(
        src_ref=src,
        dst_ref=dst,
        send_sem=send_sem,
        recv_sem=recv_sem,
        device_id=where,
        device_id_type=MESH,
    )


def tiled_dot_t(left_ref, w_ref, store):
    tile = 256
    left = left_ref[...]

    def step(index, carry):
        start = pl.multiple_of(index * tile, tile)
        store(start, tile, dot_t(left, w_ref[pl.ds(start, tile), :]).astype(BF16))
        return carry

    lax.fori_loop(0, w_ref.shape[0] // tile, step, 0)


def opening_body(
    n, x_ref, cot_ref, w_ref, x_out, resp_out, cot_in, w_in, part, inbox,
    x_send, x_recv, cot_sems, w_sem, part_send, part_recv, own_sem, turn_sem,
):
    d, sec, t = lax.axis_index("dp"), lax.axis_index("section"), lax.axis_index("tensor")
    crossing = jnp.where(d == t, 0, 1)
    for k in range(1, n):
        greet(at(d, sec, lax.rem(t + k, n)))
        greet(at(lax.rem(d + k, n), sec, t))
    greet(at(d, 1 - sec, t))

    @pl.when(d != t)
    def _():
        greet(at(t, sec, d))

    pl.semaphore_wait(pltpu.get_barrier_semaphore(), 2 * n - 1 + crossing)

    own = pltpu.make_async_copy(x_ref, x_out.at[t], own_sem)
    own.start()

    @pl.when(sec == 0)
    def _():
        pl.semaphore_wait(turn_sem, 1)

    def pass_on(src, slot, right):
        step = 1 if right else -1
        return remote(
            src, x_out.at[slot], x_send.at[slot, int(right)], x_recv.at[slot],
            at(d, sec, t + step),
        )

    @pl.when(t + 1 < n)
    def _():
        pass_on(x_ref, t, True).start()

    @pl.when(t > 0)
    def _():
        pass_on(x_ref, t, False).start()

    @pl.when(sec == 1)
    def _():
        load = pltpu.make_async_copy(w_ref, w_in, w_sem)
        load.start()
        swap = remote(cot_ref, cot_in, cot_sems.at[0], cot_sems.at[1], at(t, sec, d))
        keep = pltpu.make_async_copy(cot_ref, cot_in, cot_sems.at[2])

        @pl.when(d != t)
        def _():
            swap.start()
            swap.wait()

        @pl.when(d == t)
        def _():
            keep.start()
            keep.wait()

        load.wait()

        def store(start, size, value):
            part[:, pl.ds(start, size)] = value

        tiled_dot_t(cot_in, w_in, store)
        for k in range(1, n):
            remote(
                part, inbox.at[d], part_send.at[k], part_recv.at[d],
                at(lax.rem(d + k, n), sec, t),
            ).start()

    for k in range(1, n):
        left, right = t - k, t + k

        @pl.when(left >= 0)
        def _():
            pass_on(x_ref, left, True).wait_recv()

            @pl.when(t + 1 < n)
            def _():
                pass_on(x_out.at[left], left, True).start()

        @pl.when(right < n)
        def _():
            pass_on(x_ref, right, False).wait_recv()

            @pl.when(t > 0)
            def _():
                pass_on(x_out.at[right], right, False).start()

    own.wait()

    @pl.when(sec == 1)
    def _():
        pl.semaphore_signal(turn_sem, inc=1, device_id=at(d, 0, t), device_id_type=MESH)
        total = part[...].astype(F32)
        for k in range(1, n):
            peer = lax.rem(d + k, n)
            move = remote(
                part, inbox.at[peer], part_send.at[k], part_recv.at[peer], at(peer, sec, t)
            )
            move.wait_recv()
            total = total + inbox[peer].astype(F32)
        resp_out[...] = total.astype(BF16)
        for k in range(1, n):
            peer = lax.rem(d + k, n)
            remote(
                part, inbox.at[d], part_send.at[k], part_recv.at[d], at(peer, sec, t)
            ).wait_send()

    for k in range(n):
        left, right = t - k, t + k

        @pl.when((left >= 0) & (t + 1 < n))
        def _():
            pass_on(x_ref, left, True).wait_send()

        @pl.when((right < n) & (t > 0))
        def _():
            pass_on(x_ref, right, False).wait_send()


def opening(n, x, cot, w):
    many, wide = x.shape
    resp = cot.shape[0]
    cols = w.shape[0]
    dma = pltpu.SemaphoreType.DMA
    return pl.pallas_call(
        functools.partial(opening_body, n),
        in_specs=[pl.BlockSpec(memory_space=pl.ANY)] * 3,
        out_specs=[
            pl.BlockSpec(memory_space=pl.ANY),
            pl.BlockSpec(memory_space=pltpu.VMEM),
        ],
        out_shape=[
            jax.ShapeDtypeStruct((n, many, wide), BF16),
            jax.ShapeDtypeStruct((resp, cols), BF16),
        ],
        scratch_shapes=[
            pltpu.VMEM((resp, wide), BF16),
            pltpu.VMEM(w.shape, BF16),
            pltpu.VMEM((resp, cols), BF16),
            pltpu.VMEM((n, resp, cols), BF16),
            dma((n, 2)),
            dma((n,)),
            dma((3,)),
            dma,
            dma((n,)),
            dma((n,)),
            dma,
            pltpu.SemaphoreType.REGULAR,
        ],
        compiler_params=pltpu.CompilerParams(
            collective_id=0, has_side_effects=True, vmem_limit_bytes=BIG
        ),
    )(x, cot, w)


def finish_body(
    n, active, width, part_ref, x_ref, up_ref, gain_ref, rms_ref, out_ref, low_ref,
    inbox, stats, send, recv, stat_send, stat_recv, own_sem,
):
    d, sec, t = lax.axis_index("dp"), lax.axis_index("section"), lax.axis_index("tensor")
    many, wide = x_ref.shape
    tile = 16
    for k in range(1, n):
        greet(at(d, sec, lax.rem(t + k, n)))
    pl.semaphore_wait(pltpu.get_barrier_semaphore(), n - 1)

    def block(j):
        return part_ref.at[:, pl.ds(pl.multiple_of(j * wide, wide), wide)]

    @pl.when(sec == active)
    def _():
        own = pltpu.make_async_copy(block(t), inbox.at[t], own_sem)
        own.start()

        def push(k):
            peer = lax.rem(t + k, n)
            return remote(
                block(peer), inbox.at[t], send.at[k], recv.at[t], at(d, sec, peer)
            )

        for k in range(1, n):
            push(k).start()
        own.wait()
        for k in range(1, n):
            peer = lax.rem(t + k, n)
            remote(
                block(peer), inbox.at[peer], send.at[k], recv.at[peer], at(d, sec, peer)
            ).wait_recv()

        def gather_sum(index, carry):
            rows = pl.ds(pl.multiple_of(index * tile, tile), tile)
            total = inbox[0, rows, :].astype(F32)
            for j in range(1, n):
                total = total + inbox[j, rows, :].astype(F32)
            scaled = total * gain_ref[...]
            out_ref[rows, :] = scaled
            dots = jnp.sum(x_ref[rows, :].astype(F32) * scaled, -1, keepdims=True)
            stats[t, rows, :] = jnp.broadcast_to(dots, (tile, HD))
            return carry

        lax.fori_loop(0, many // tile, gather_sum, 0)

        for k in range(1, n):
            peer = lax.rem(t + k, n)
            remote(
                stats.at[t], stats.at[t], stat_send.at[k], stat_recv.at[t], at(d, sec, peer)
            ).start()
        for k in range(1, n):
            peer = lax.rem(t + k, n)
            remote(
                stats.at[peer], stats.at[peer], stat_send.at[k], stat_recv.at[peer],
                at(d, sec, peer),
            ).wait_recv()

        def settle(index, carry):
            rows = pl.ds(pl.multiple_of(index * tile, tile), tile)
            stat = stats[0, rows, :]
            for j in range(1, n):
                stat = stat + stats[j, rows, :]
            rms = rms_ref[rows, :]
            factor = (rms * rms * rms * stat / width)[:, :1]
            value = (
                up_ref[rows, :].astype(F32)
                + rms[:, :1] * out_ref[rows, :]
                - x_ref[rows, :].astype(F32) * factor
            )
            out_ref[rows, :] = value
            low_ref[rows, :] = value.astype(BF16)
            return carry

        lax.fori_loop(0, many // tile, settle, 0)
        for k in range(1, n):
            push(k).wait_send()
            peer = lax.rem(t + k, n)
            remote(
                stats.at[t], stats.at[t], stat_send.at[k], stat_recv.at[t], at(d, sec, peer)
            ).wait_send()


def finish(n, active, part, x, up, gain, rms):
    many, wide = x.shape
    dma = pltpu.SemaphoreType.DMA
    vmem = pl.BlockSpec(memory_space=pltpu.VMEM)
    return pl.pallas_call(
        functools.partial(finish_body, n, active, part.shape[1]),
        in_specs=[pl.BlockSpec(memory_space=pl.ANY)] + [vmem] * 4,
        out_specs=[vmem, vmem],
        out_shape=[
            jax.ShapeDtypeStruct((many, wide), F32),
            jax.ShapeDtypeStruct((many, wide), BF16),
        ],
        scratch_shapes=[
            pltpu.VMEM((n, many, wide), BF16),
            pltpu.VMEM((n, many, HD), F32),
            dma((n,)),
            dma((n,)),
            dma((n,)),
            dma((n,)),
            dma,
        ],
        compiler_params=pltpu.CompilerParams(
            collective_id=1 + active, has_side_effects=True, vmem_limit_bytes=BIG
        ),
    )(part, x, up, gain, rms)


def descend_body(
    n, g_ref, w_ref, up_out, go_out, mid, spread, w_in, outbox, inbox,
    g_send, g_recv, s_send, s_recv, p_send, p_recv, w_sem, up_sem,
):
    d, sec, t = lax.axis_index("dp"), lax.axis_index("section"), lax.axis_index("tensor")
    for k in range(n):
        greet(at(d, 1 - sec, lax.rem(t + k, n)))

    @pl.when(sec == 0)
    def _():
        for k in range(1, n):
            greet(at(lax.rem(d + k, n), sec, t))

    pl.semaphore_wait(pltpu.get_barrier_semaphore(), n + (1 - sec) * (n - 1))

    def hand(k):
        return remote(
            g_ref, mid.at[t], g_send.at[k], g_recv.at[t], at(d, 0, lax.rem(t + k, n))
        )

    @pl.when(sec == 1)
    def _():
        for k in range(n):
            hand(k).start()
        for k in range(n):
            hand(k).wait_send()

    @pl.when(sec == 0)
    def _():
        load = pltpu.make_async_copy(w_ref, w_in, w_sem)
        load.start()

        def arrived(slot):
            remote(
                mid.at[slot], mid.at[slot], g_send.at[0], g_recv.at[slot], at(d, 1, slot)
            ).wait_recv()

        def move(k):
            peer = lax.rem(d + k, n)
            return remote(
                mid.at[peer], spread.at[d], s_send.at[k], s_recv.at[d], at(peer, 0, t)
            )

        for k in range(1, n):
            arrived(lax.rem(d + k, n))
            move(k).start()
        arrived(d)
        keep = pltpu.make_async_copy(mid.at[t], up_out, up_sem)
        keep.start()
        load.wait()

        def give(k):
            peer = lax.rem(d + k, n)
            return remote(
                outbox.at[peer], inbox.at[d], p_send.at[k], p_recv.at[d], at(peer, 0, t)
            )

        for k in range(1, n):
            peer = lax.rem(d + k, n)
            remote(
                spread.at[peer], spread.at[peer], s_send.at[k], s_recv.at[peer],
                at(peer, 0, t),
            ).wait_recv()

            def store(start, size, value):
                outbox[peer, :, pl.ds(start, size)] = value

            tiled_dot_t(spread.at[peer], w_in, store)
            give(k).start()

        def store_own(start, size, value):
            outbox[d, :, pl.ds(start, size)] = value

        tiled_dot_t(mid.at[d], w_in, store_own)
        for k in range(1, n):
            peer = lax.rem(d + k, n)
            remote(
                inbox.at[peer], inbox.at[peer], p_send.at[k], p_recv.at[peer],
                at(peer, 0, t),
            ).wait_recv()
        tile = 16

        def add(index, carry):
            rows = pl.ds(pl.multiple_of(index * tile, tile), tile)
            total = outbox[d, rows, :].astype(F32)
            for k in range(1, n):
                total = total + inbox[lax.rem(d + k, n), rows, :].astype(F32)
            go_out[rows, :] = total.astype(BF16)
            return carry

        lax.fori_loop(0, go_out.shape[0] // tile, add, 0)
        keep.wait()
        for k in range(1, n):
            move(k).wait_send()
            give(k).wait_send()


def descend(n, g, w):
    many, wide = g.shape
    cols = w.shape[0]
    dma = pltpu.SemaphoreType.DMA
    vmem = pl.BlockSpec(memory_space=pltpu.VMEM)
    return pl.pallas_call(
        functools.partial(descend_body, n),
        in_specs=[vmem, pl.BlockSpec(memory_space=pl.ANY)],
        out_specs=[vmem, vmem],
        out_shape=[
            jax.ShapeDtypeStruct((many, wide), BF16),
            jax.ShapeDtypeStruct((many, cols), BF16),
        ],
        scratch_shapes=[
            pltpu.VMEM((n, many, wide), BF16),
            pltpu.VMEM((n, many, wide), BF16),
            pltpu.VMEM(w.shape, BF16),
            pltpu.VMEM((n, many, cols), BF16),
            pltpu.VMEM((n, many, cols), BF16),
            dma((n,)),
            dma((n,)),
            dma((n,)),
            dma((n,)),
            dma((n,)),
            dma((n,)),
            dma,
            dma,
        ],
        compiler_params=pltpu.CompilerParams(
            collective_id=3, has_side_effects=True, vmem_limit_bytes=BIG
        ),
    )(g, w)


def on_device(
    n_tensor, stored, cotangent, positions, lengths, norm_gain, w_query, w_key, w_value, w_out
):
    x_own = stored[0]
    gain = norm_gain[0]
    w_q, w_k, w_v, w_o = w_query[0], w_key[0], w_value[0], w_out[0]
    seqs, rows, width_dev = x_own.shape
    many = seqs * rows
    width = gain.shape[0]
    kv_cols = w_k.shape[1]
    dp_id = lax.axis_index("dp")
    tensor_id = lax.axis_index("tensor")
    section_id = lax.axis_index("section")
    row_ids = dp_id * rows + jnp.arange(rows, dtype=jnp.int32)
    cosine, sine = angle_tables(row_ids.astype(F32))
    lens = jnp.stack(
        [lengths, jnp.full_like(lengths, dp_id * rows)], 0
    )

    resp = cotangent.shape[1]
    x_parts, resp_grad = opening(
        n_tensor,
        x_own.reshape(many, width_dev),
        cotangent.reshape(seqs * resp, width_dev),
        w_o,
    )
    resp_grad = resp_grad.reshape(seqs, resp, -1)
    placed = (positions[:, None, :] == row_ids[None, :, None]).astype(BF16)

    def place(small):
        return jnp.einsum("spr,srd->spd", placed, small, preferred_element_type=F32).astype(BF16)

    squares = jnp.sum(jnp.square(x_parts.astype(F32)), (0, 2))[:, None]
    inv_rms = lax.rsqrt(squares / width + EPS)
    normed = jnp.concatenate(
        [
            (
                x_parts[part].astype(F32)
                * inv_rms
                * gain[part * width_dev : (part + 1) * width_dev]
            ).astype(BF16)
            for part in range(n_tensor)
        ],
        1,
    )
    queries, keys, values = lax.optimization_barrier(
        (dot_n(normed, w_q), dot_n(normed, w_k), dot_n(normed, w_v))
    )
    k_four = keys.reshape(seqs, rows, -1, HD)
    k_rot = k_four * cosine[:, None] + turn_plain(k_four) * sine[:, None]
    kv_own = jnp.concatenate(
        [k_rot.reshape(seqs, rows, kv_cols), values.reshape(seqs, rows, kv_cols)], -1
    ).astype(BF16)
    kv_all = lax.all_gather(kv_own, "dp", axis=1, tiled=True)
    k_all, v_all = kv_all[..., :kv_cols], kv_all[..., kv_cols:]
    queries = queries.reshape(seqs, rows, -1)
    gain_own = lax.dynamic_slice_in_dim(gain, tensor_id * width_dev, width_dev, 0)
    x_mine = x_own.reshape(many, width_dev)
    rms_wide = jnp.broadcast_to(inv_rms, (many, HD))

    def backward(active, upstream_own, grad_out):
        grad_q, key_terms, value_terms = attention_grad(
            lens, queries, grad_out, k_all, v_all, cosine, sine
        )
        kv_sum = lax.psum_scatter(
            jnp.concatenate([key_terms, value_terms], -1), "dp", scatter_dimension=1, tiled=True
        ).astype(F32)
        gk_four = kv_sum[..., :kv_cols].reshape(seqs, rows, -1, HD)
        grad_k = gk_four * cosine[:, None] - turn_plain(gk_four) * sine[:, None]
        grad_k = grad_k.astype(BF16).reshape(many, kv_cols)
        grad_v = kv_sum[..., kv_cols:].astype(BF16).reshape(many, kv_cols)
        partial = dot_t(grad_q.reshape(many, -1), w_q) + dot_t(grad_k, w_k) + dot_t(grad_v, w_v)
        return finish(
            n_tensor,
            active,
            partial.astype(BF16),
            x_mine,
            upstream_own.reshape(many, width_dev),
            gain_own[None],
            rms_wide,
        )

    first, first_low = backward(1, place(cotangent), place(resp_grad))

    handed, grad_out = descend(n_tensor, first_low, w_o)
    second, _ = backward(0, handed, grad_out.reshape(seqs, rows, -1))
    result = jnp.where(section_id == 0, second, first)
    return result.reshape(1, seqs, rows, width_dev)


def solution(mesh):
    return jax.shard_map(
        functools.partial(on_device, mesh.shape["tensor"]),
        mesh=mesh,
        in_specs=(
            P("section", None, "dp", "tensor"),
            P(None, None, "tensor"),
            P(),
            P(),
            P("section", None),
            P("section", None, "tensor"),
            P("section", None, "tensor"),
            P("section", None, "tensor"),
            P("section", "tensor", "dp"),
        ),
        out_specs=P("section", None, "dp", "tensor"),
        check_vma=False,
    )
```

```python
import functools
import math

import jax
import jax.numpy as jnp
from jax import lax
from jax.experimental import pallas as pl
from jax.experimental.pallas import tpu as pltpu
from jax.sharding import PartitionSpec as P

HD = 128
EPS = 1e-05
THETA = 500000.0
F32 = jnp.float32
BF16 = jnp.bfloat16


def dot_t(left, right):
    return lax.dot_general(left, right, (((1,), (1,)), ((), ())), preferred_element_type=F32)


def dot_n(left, right):
    return lax.dot_general(left, right, (((1,), (0,)), ((), ())), preferred_element_type=F32)


def dot_c(left, right):
    return lax.dot_general(left, right, (((0,), (0,)), ((), ())), preferred_element_type=F32)


def angle_tables(row_places):
    half_dim = HD // 2
    frequency = THETA ** (-(jnp.arange(half_dim, dtype=F32) * 2.0) / HD)
    angles = row_places[:, None] * frequency[None, :]
    cosine = jnp.concatenate([jnp.cos(angles), jnp.cos(angles)], -1)
    signed_sine = jnp.concatenate([-jnp.sin(angles), jnp.sin(angles)], -1)
    return cosine, signed_sine


def turn_plain(values):
    half_dim = HD // 2
    return jnp.concatenate([values[..., half_dim:], values[..., :half_dim]], -1)


MESH = pl.DeviceIdType.MESH
BIG = 56 * 1024 * 1024


def at(dp, section, tensor):
    return {"dp": dp, "section": section, "tensor": tensor}


def greet(where):
    pl.semaphore_signal(
        pltpu.get_barrier_semaphore(), inc=1, device_id=where, device_id_type=MESH
    )


def remote(src, dst, send_sem, recv_sem, where):
    return pltpu.make_async_remote_copy(
        src_ref=src,
        dst_ref=dst,
        send_sem=send_sem,
        recv_sem=recv_sem,
        device_id=where,
        device_id_type=MESH,
    )


def tiled_dot_t(left_ref, w_ref, store):
    tile = 256
    left = left_ref[...]

    def step(index, carry):
        start = pl.multiple_of(index * tile, tile)
        store(start, tile, dot_t(left, w_ref[pl.ds(start, tile), :]).astype(BF16))
        return carry

    lax.fori_loop(0, w_ref.shape[0] // tile, step, 0)


def opening_body(
    n, x_ref, cot_ref, w_ref, x_out, resp_out, cot_in, w_in, part, inbox,
    x_send, x_recv, cot_sems, w_sem, part_send, part_recv, own_sem, turn_sem,
):
    d, sec, t = lax.axis_index("dp"), lax.axis_index("section"), lax.axis_index("tensor")
    crossing = jnp.where(d == t, 0, 1)
    for k in range(1, n):
        greet(at(d, sec, lax.rem(t + k, n)))
        greet(at(lax.rem(d + k, n), sec, t))
    greet(at(d, 1 - sec, t))

    @pl.when(d != t)
    def _():
        greet(at(t, sec, d))

    pl.semaphore_wait(pltpu.get_barrier_semaphore(), 2 * n - 1 + crossing)

    own = pltpu.make_async_copy(x_ref, x_out.at[t], own_sem)
    own.start()

    @pl.when(sec == 0)
    def _():
        pl.semaphore_wait(turn_sem, 1)

    def pass_on(src, slot, right):
        step = 1 if right else -1
        return remote(
            src, x_out.at[slot], x_send.at[slot, int(right)], x_recv.at[slot],
            at(d, sec, t + step),
        )

    @pl.when(t + 1 < n)
    def _():
        pass_on(x_ref, t, True).start()

    @pl.when(t > 0)
    def _():
        pass_on(x_ref, t, False).start()

    load = pltpu.make_async_copy(w_ref, w_in, w_sem)
    swap = remote(cot_ref, cot_in, cot_sems.at[0], cot_sems.at[1], at(t, sec, d))
    keep = pltpu.make_async_copy(cot_ref, cot_in, cot_sems.at[2])

    @pl.when(sec == 1)
    def _():
        load.start()

        @pl.when(d != t)
        def _():
            swap.start()

        @pl.when(d == t)
        def _():
            keep.start()

    def respond():
        @pl.when(d != t)
        def _():
            swap.wait()

        @pl.when(d == t)
        def _():
            keep.wait()

        load.wait()

        def store(start, size, value):
            part[:, pl.ds(start, size)] = value

        tiled_dot_t(cot_in, w_in, store)
        for k in range(1, n):
            remote(
                part, inbox.at[d], part_send.at[k], part_recv.at[d],
                at(lax.rem(d + k, n), sec, t),
            ).start()

    for k in range(1, n):
        left, right = t - k, t + k

        @pl.when(left >= 0)
        def _():
            pass_on(x_ref, left, True).wait_recv()

            @pl.when(t + 1 < n)
            def _():
                pass_on(x_out.at[left], left, True).start()

        @pl.when(right < n)
        def _():
            pass_on(x_ref, right, False).wait_recv()

            @pl.when(t > 0)
            def _():
                pass_on(x_out.at[right], right, False).start()

        if k == 1:
            pl.when(sec == 1)(respond)

    own.wait()

    @pl.when(sec == 1)
    def _():
        pl.semaphore_signal(turn_sem, inc=1, device_id=at(d, 0, t), device_id_type=MESH)
        total = part[...].astype(F32)
        for k in range(1, n):
            peer = lax.rem(d + k, n)
            move = remote(
                part, inbox.at[peer], part_send.at[k], part_recv.at[peer], at(peer, sec, t)
            )
            move.wait_recv()
            total = total + inbox[peer].astype(F32)
        resp_out[...] = total.astype(BF16)
        for k in range(1, n):
            peer = lax.rem(d + k, n)
            remote(
                part, inbox.at[d], part_send.at[k], part_recv.at[d], at(peer, sec, t)
            ).wait_send()

    for k in range(n):
        left, right = t - k, t + k

        @pl.when((left >= 0) & (t + 1 < n))
        def _():
            pass_on(x_ref, left, True).wait_send()

        @pl.when((right < n) & (t > 0))
        def _():
            pass_on(x_ref, right, False).wait_send()


def opening(n, x, cot, w):
    many, wide = x.shape
    resp = cot.shape[0]
    cols = w.shape[0]
    dma = pltpu.SemaphoreType.DMA
    return pl.pallas_call(
        functools.partial(opening_body, n),
        in_specs=[pl.BlockSpec(memory_space=pl.ANY)] * 3,
        out_specs=[
            pl.BlockSpec(memory_space=pl.ANY),
            pl.BlockSpec(memory_space=pltpu.VMEM),
        ],
        out_shape=[
            jax.ShapeDtypeStruct((n, many, wide), BF16),
            jax.ShapeDtypeStruct((resp, cols), BF16),
        ],
        scratch_shapes=[
            pltpu.VMEM((resp, wide), BF16),
            pltpu.VMEM(w.shape, BF16),
            pltpu.VMEM((resp, cols), BF16),
            pltpu.VMEM((n, resp, cols), BF16),
            dma((n, 2)),
            dma((n,)),
            dma((3,)),
            dma,
            dma((n,)),
            dma((n,)),
            dma,
            pltpu.SemaphoreType.REGULAR,
        ],
        compiler_params=pltpu.CompilerParams(
            collective_id=0, has_side_effects=True, vmem_limit_bytes=BIG
        ),
    )(x, cot, w)


def finish_body(
    n, active, width, gq_ref, gkv_ref, x_ref, up_ref, gain_ref, rms_ref, wq_ref, wk_ref, wv_ref,
    out_ref, low_ref, inbox, outbox, stats, wq_in, wk_in, wv_in, w_sems,
    send, recv, stat_send, stat_recv,
):
    d, sec, t = lax.axis_index("dp"), lax.axis_index("section"), lax.axis_index("tensor")
    many, wide = x_ref.shape
    kv_cols = wk_in.shape[2]
    tile = 16
    deep = wq_in.shape[1]
    per = wide // deep

    for k in range(1, n):
        greet(at(d, sec, lax.rem(t + k, n)))
    pl.semaphore_wait(pltpu.get_barrier_semaphore(), n - 1)

    @pl.when(sec == active)
    def _():
        def loads(count):
            owner = lax.rem(t + 1 + count // per, n)
            rows = pl.ds(pl.multiple_of(owner * wide + lax.rem(count, per) * deep, deep), deep)
            slot = lax.rem(count, 2)
            return [
                pltpu.make_async_copy(source.at[rows, :], into.at[slot], w_sems.at[slot, which])
                for which, (source, into) in enumerate(
                    ((wq_ref, wq_in), (wk_ref, wk_in), (wv_ref, wv_in))
                )
            ]

        def push(k):
            peer = lax.rem(t + k, n)
            return remote(
                outbox.at[peer], inbox.at[t], send.at[k], recv.at[t], at(d, sec, peer)
            )

        for load in loads(jnp.int32(0)):
            load.start()
        for k in range(1, n + 1):
            owner = lax.rem(t + k, n)

            def project(index, carry):
                count = (k - 1) * per + index

                @pl.when(count + 1 < n * per)
                def _():
                    for load in loads(count + 1):
                        load.start()

                for load in loads(count):
                    load.wait()
                slot = lax.rem(count, 2)
                value = (
                    dot_t(gq_ref[...], wq_in[slot])
                    + dot_t(gkv_ref[:, :kv_cols], wk_in[slot])
                    + dot_t(gkv_ref[:, kv_cols:], wv_in[slot])
                ).astype(BF16)
                columns = pl.ds(pl.multiple_of(index * deep, deep), deep)
                if k < n:
                    outbox[owner, :, columns] = value
                else:
                    inbox[owner, :, columns] = value
                return carry

            lax.fori_loop(0, per, project, 0)
            if k < n:
                push(k).start()

        for k in range(1, n):
            peer = lax.rem(t + k, n)
            remote(
                outbox.at[peer], inbox.at[peer], send.at[k], recv.at[peer], at(d, sec, peer)
            ).wait_recv()

        def gather_sum(index, carry):
            rows = pl.ds(pl.multiple_of(index * tile, tile), tile)
            total = inbox[0, rows, :].astype(F32)
            for j in range(1, n):
                total = total + inbox[j, rows, :].astype(F32)
            scaled = total * gain_ref[...]
            out_ref[rows, :] = scaled
            dots = jnp.sum(x_ref[rows, :].astype(F32) * scaled, -1, keepdims=True)
            stats[t, rows, :] = jnp.broadcast_to(dots, (tile, HD))
            return carry

        lax.fori_loop(0, many // tile, gather_sum, 0)

        for k in range(1, n):
            peer = lax.rem(t + k, n)
            remote(
                stats.at[t], stats.at[t], stat_send.at[k], stat_recv.at[t], at(d, sec, peer)
            ).start()
        for k in range(1, n):
            peer = lax.rem(t + k, n)
            remote(
                stats.at[peer], stats.at[peer], stat_send.at[k], stat_recv.at[peer],
                at(d, sec, peer),
            ).wait_recv()

        def settle(index, carry):
            rows = pl.ds(pl.multiple_of(index * tile, tile), tile)
            stat = stats[0, rows, :]
            for j in range(1, n):
                stat = stat + stats[j, rows, :]
            rms = rms_ref[rows, :]
            factor = (rms * rms * rms * stat / width)[:, :1]
            value = (
                up_ref[rows, :].astype(F32)
                + rms[:, :1] * out_ref[rows, :]
                - x_ref[rows, :].astype(F32) * factor
            )
            out_ref[rows, :] = value
            low_ref[rows, :] = value.astype(BF16)
            return carry

        lax.fori_loop(0, many // tile, settle, 0)
        for k in range(1, n):
            push(k).wait_send()
            peer = lax.rem(t + k, n)
            remote(
                stats.at[t], stats.at[t], stat_send.at[k], stat_recv.at[t], at(d, sec, peer)
            ).wait_send()


def finish(n, active, gq, gkv, x, up, gain, rms, wq, wk, wv):
    many, wide = x.shape
    deep = 512
    dma = pltpu.SemaphoreType.DMA
    vmem = pl.BlockSpec(memory_space=pltpu.VMEM)
    return pl.pallas_call(
        functools.partial(finish_body, n, active, wq.shape[0]),
        in_specs=[vmem] * 6 + [pl.BlockSpec(memory_space=pl.ANY)] * 3,
        out_specs=[vmem, vmem],
        out_shape=[
            jax.ShapeDtypeStruct((many, wide), F32),
            jax.ShapeDtypeStruct((many, wide), BF16),
        ],
        scratch_shapes=[
            pltpu.VMEM((n, many, wide), BF16),
            pltpu.VMEM((n, many, wide), BF16),
            pltpu.VMEM((n, many, HD), F32),
            pltpu.VMEM((2, deep, wq.shape[1]), BF16),
            pltpu.VMEM((2, deep, wk.shape[1]), BF16),
            pltpu.VMEM((2, deep, wv.shape[1]), BF16),
            dma((2, 3)),
            dma((n,)),
            dma((n,)),
            dma((n,)),
            dma((n,)),
        ],
        compiler_params=pltpu.CompilerParams(
            collective_id=1 + active, has_side_effects=True, vmem_limit_bytes=BIG
        ),
    )(gq, gkv, x, up, gain, rms, wq, wk, wv)


def descend_body(
    n, g_ref, w_ref, up_out, go_out, mid, spread, w_in, outbox, inbox,
    g_send, g_recv, s_send, s_recv, p_send, p_recv, w_sem, up_sem,
):
    d, sec, t = lax.axis_index("dp"), lax.axis_index("section"), lax.axis_index("tensor")
    for k in range(n):
        greet(at(d, 1 - sec, lax.rem(t + k, n)))

    @pl.when(sec == 0)
    def _():
        for k in range(1, n):
            greet(at(lax.rem(d + k, n), sec, t))

    pl.semaphore_wait(pltpu.get_barrier_semaphore(), n + (1 - sec) * (n - 1))

    def hand(k):
        return remote(
            g_ref, mid.at[t], g_send.at[k], g_recv.at[t], at(d, 0, lax.rem(t + k, n))
        )

    @pl.when(sec == 1)
    def _():
        for k in range(n):
            hand(k).start()
        for k in range(n):
            hand(k).wait_send()

    @pl.when(sec == 0)
    def _():
        load = pltpu.make_async_copy(w_ref, w_in, w_sem)
        load.start()

        def arrived(slot):
            remote(
                mid.at[slot], mid.at[slot], g_send.at[0], g_recv.at[slot], at(d, 1, slot)
            ).wait_recv()

        def move(k):
            peer = lax.rem(d + k, n)
            return remote(
                mid.at[peer], spread.at[d], s_send.at[k], s_recv.at[d], at(peer, 0, t)
            )

        for k in range(1, n):
            arrived(lax.rem(d + k, n))
            move(k).start()
        arrived(d)
        keep = pltpu.make_async_copy(mid.at[t], up_out, up_sem)
        keep.start()
        load.wait()

        def give(k):
            peer = lax.rem(d + k, n)
            return remote(
                outbox.at[peer], inbox.at[d], p_send.at[k], p_recv.at[d], at(peer, 0, t)
            )

        for k in range(1, n):
            peer = lax.rem(d + k, n)
            remote(
                spread.at[peer], spread.at[peer], s_send.at[k], s_recv.at[peer],
                at(peer, 0, t),
            ).wait_recv()

            def store(start, size, value):
                outbox[peer, :, pl.ds(start, size)] = value

            tiled_dot_t(spread.at[peer], w_in, store)
            give(k).start()

        def store_own(start, size, value):
            outbox[d, :, pl.ds(start, size)] = value

        tiled_dot_t(mid.at[d], w_in, store_own)
        for k in range(1, n):
            peer = lax.rem(d + k, n)
            remote(
                inbox.at[peer], inbox.at[peer], p_send.at[k], p_recv.at[peer],
                at(peer, 0, t),
            ).wait_recv()
        tile = 16

        def add(index, carry):
            rows = pl.ds(pl.multiple_of(index * tile, tile), tile)
            total = outbox[d, rows, :].astype(F32)
            for k in range(1, n):
                total = total + inbox[lax.rem(d + k, n), rows, :].astype(F32)
            go_out[rows, :] = total.astype(BF16)
            return carry

        lax.fori_loop(0, go_out.shape[0] // tile, add, 0)
        keep.wait()
        for k in range(1, n):
            move(k).wait_send()
            give(k).wait_send()


def descend(n, g, w):
    many, wide = g.shape
    cols = w.shape[0]
    dma = pltpu.SemaphoreType.DMA
    vmem = pl.BlockSpec(memory_space=pltpu.VMEM)
    return pl.pallas_call(
        functools.partial(descend_body, n),
        in_specs=[vmem, pl.BlockSpec(memory_space=pl.ANY)],
        out_specs=[vmem, vmem],
        out_shape=[
            jax.ShapeDtypeStruct((many, wide), BF16),
            jax.ShapeDtypeStruct((many, cols), BF16),
        ],
        scratch_shapes=[
            pltpu.VMEM((n, many, wide), BF16),
            pltpu.VMEM((n, many, wide), BF16),
            pltpu.VMEM(w.shape, BF16),
            pltpu.VMEM((n, many, cols), BF16),
            pltpu.VMEM((n, many, cols), BF16),
            dma((n,)),
            dma((n,)),
            dma((n,)),
            dma((n,)),
            dma((n,)),
            dma((n,)),
            dma,
            dma,
        ],
        compiler_params=pltpu.CompilerParams(
            collective_id=3, has_side_effects=True, vmem_limit_bytes=BIG
        ),
    )(g, w)


def attend_body(n, active, gather, lens_ref, q_ref, o_ref, kv_ref, cos_ref, sin_ref, *rest):
    if gather:
        gq_ref, gkv_ref, kv_out, kv_box, terms, inbox, kv_send, kv_recv, send, recv = rest
    else:
        gq_ref, gkv_ref, terms, inbox, send, recv = rest
        kv_box = kv_ref
    d, sec, t = lax.axis_index("dp"), lax.axis_index("section"), lax.axis_index("tensor")
    batch, rows, cols = q_ref.shape
    kv_cols = kv_box.shape[3] // 2
    kv_dev = kv_cols // HD
    group = cols // kv_cols
    length = n * rows
    many = rows * group
    scale = 1.0 / math.sqrt(HD)
    for k in range(1, n):
        greet(at(lax.rem(d + k, n), sec, t))
    pl.semaphore_wait(pltpu.get_barrier_semaphore(), n - 1)

    if gather:
        for k in range(1, n):
            remote(
                kv_ref, kv_box.at[d], kv_send.at[k], kv_recv.at[d],
                at(lax.rem(d + k, n), sec, t),
            ).start()
        kv_box[d] = kv_ref[...]
        for k in range(1, n):
            peer = lax.rem(d + k, n)
            remote(
                kv_ref, kv_box.at[peer], kv_send.at[k], kv_recv.at[peer], at(peer, sec, t)
            ).wait_recv()
        kv_out[...] = kv_box[...]

    @pl.when(sec == active)
    def _():
        cosine, sine = cos_ref[...], sin_ref[...]

        def one(index, carry):
            seq = index // kv_dev
            kv_head = lax.rem(index, kv_dev)
            k_lanes = pl.ds(pl.multiple_of(kv_head * HD, HD), HD)
            v_lanes = pl.ds(pl.multiple_of(kv_cols + kv_head * HD, HD), HD)

            def q_lanes(head):
                return pl.ds(pl.multiple_of((kv_head * group + head) * HD, HD), HD)

            q_parts, o_parts = [], []
            for head in range(group):
                raw = q_ref[seq, :, q_lanes(head)]
                turned = raw * cosine + pltpu.roll(raw, HD // 2, 1) * sine
                q_parts.append(turned.astype(BF16))
                o_parts.append(o_ref[seq, :, q_lanes(head)])
            q_all = jnp.concatenate(q_parts, 0)
            o_all = jnp.concatenate(o_parts, 0)
            keys = jnp.concatenate([kv_box[r, seq, :, k_lanes] for r in range(n)], 0)
            values = jnp.concatenate([kv_box[r, seq, :, v_lanes] for r in range(n)], 0)
            row_at = lax.broadcasted_iota(jnp.int32, (many, length), 0) & (rows - 1)
            query_at = d * rows + row_at
            key_at = lax.broadcasted_iota(jnp.int32, (many, length), 1)
            start = length - lens_ref[seq]
            allowed = (key_at == query_at) | ((key_at < query_at) & (key_at >= start))
            scores = jnp.where(allowed, dot_t(q_all, keys) * scale, -1e30)
            highest = jnp.max(scores, -1, keepdims=True)
            terms_e = jnp.where(allowed, jnp.exp(scores - highest), 0.0)
            probs = terms_e / jnp.sum(terms_e, -1, keepdims=True)
            grad_probs = dot_t(o_all, values)
            row_dot = jnp.sum(probs * grad_probs, -1, keepdims=True)
            grad_scores = (probs * (grad_probs - row_dot) * scale).astype(BF16)
            grad_qr = dot_n(grad_scores, keys)
            grad_k = dot_c(grad_scores, q_all).astype(BF16)
            grad_v = dot_c(probs.astype(BF16), o_all).astype(BF16)
            for r in range(n):
                terms[r, seq, :, k_lanes] = grad_k[r * rows : (r + 1) * rows]
                terms[r, seq, :, v_lanes] = grad_v[r * rows : (r + 1) * rows]
            for head in range(group):
                part = grad_qr[head * rows : (head + 1) * rows]
                turned = part * cosine - pltpu.roll(part, HD // 2, 1) * sine
                gq_ref[seq, :, q_lanes(head)] = turned.astype(BF16)
            return carry

        lax.fori_loop(0, batch * kv_dev, one, 0)

        def push(k):
            peer = lax.rem(d + k, n)
            return remote(
                terms.at[peer], inbox.at[d], send.at[k], recv.at[d], at(peer, sec, t)
            )

        for k in range(1, n):
            push(k).start()
        inbox[d] = terms[d]
        for k in range(1, n):
            peer = lax.rem(d + k, n)
            remote(
                terms.at[peer], inbox.at[peer], send.at[k], recv.at[peer], at(peer, sec, t)
            ).wait_recv()
        for seq in range(batch):
            total = inbox[0, seq].astype(F32)
            for r in range(1, n):
                total = total + inbox[r, seq].astype(F32)
            for head in range(kv_dev):
                lanes = slice(head * HD, (head + 1) * HD)
                part = total[:, lanes]
                turned = part * cosine - pltpu.roll(part, HD // 2, 1) * sine
                gkv_ref[seq, :, lanes] = turned.astype(BF16)
            gkv_ref[seq, :, kv_cols:] = total[:, kv_cols:].astype(BF16)
        for k in range(1, n):
            push(k).wait_send()

    if gather:
        for k in range(1, n):
            remote(
                kv_ref, kv_box.at[d], kv_send.at[k], kv_recv.at[d],
                at(lax.rem(d + k, n), sec, t),
            ).wait_send()


def attend(n, active, gather, lengths, queries, grad_out, kv, cosine, sine):
    batch, rows, cols = queries.shape
    both = kv.shape[-1]
    dma = pltpu.SemaphoreType.DMA
    vmem = pl.BlockSpec(memory_space=pltpu.VMEM)
    whole = (n, batch, rows, both)
    out_shape = [
        jax.ShapeDtypeStruct((batch, rows, cols), BF16),
        jax.ShapeDtypeStruct((batch, rows, both), BF16),
    ]
    scratch = [pltpu.VMEM(whole, BF16), pltpu.VMEM(whole, BF16)]
    sems = [dma((n,)), dma((n,))]
    if gather:
        out_shape.append(jax.ShapeDtypeStruct(whole, BF16))
        scratch.append(pltpu.VMEM(whole, BF16))
        sems = sems + sems
    return pl.pallas_call(
        functools.partial(attend_body, n, active, gather),
        in_specs=[pl.BlockSpec(memory_space=pltpu.SMEM)] + [vmem] * 5,
        out_specs=[vmem] * len(out_shape),
        out_shape=out_shape,
        scratch_shapes=scratch + sems,
        compiler_params=pltpu.CompilerParams(
            collective_id=4 + active, has_side_effects=True, vmem_limit_bytes=BIG
        ),
    )(lengths, queries, grad_out, kv, cosine, sine)


def on_device(
    n_tensor, stored, cotangent, positions, lengths, norm_gain, w_query, w_key, w_value, w_out
):
    x_own = stored[0]
    gain = norm_gain[0]
    w_q, w_k, w_v, w_o = w_query[0], w_key[0], w_value[0], w_out[0]
    seqs, rows, width_dev = x_own.shape
    many = seqs * rows
    width = gain.shape[0]
    kv_cols = w_k.shape[1]
    dp_id = lax.axis_index("dp")
    tensor_id = lax.axis_index("tensor")
    section_id = lax.axis_index("section")
    row_ids = dp_id * rows + jnp.arange(rows, dtype=jnp.int32)
    cosine, sine = angle_tables(row_ids.astype(F32))
    resp = cotangent.shape[1]
    x_parts, resp_grad = opening(
        n_tensor,
        x_own.reshape(many, width_dev),
        cotangent.reshape(seqs * resp, width_dev),
        w_o,
    )
    resp_grad = resp_grad.reshape(seqs, resp, -1)
    placed = (positions[:, None, :] == row_ids[None, :, None]).astype(BF16)

    def place(small):
        return jnp.einsum("spr,srd->spd", placed, small, preferred_element_type=F32).astype(BF16)

    squares = jnp.sum(jnp.square(x_parts.astype(F32)), (0, 2))[:, None]
    inv_rms = lax.rsqrt(squares / width + EPS)
    normed = jnp.concatenate(
        [
            (
                x_parts[part].astype(F32)
                * inv_rms
                * gain[part * width_dev : (part + 1) * width_dev]
            ).astype(BF16)
            for part in range(n_tensor)
        ],
        1,
    )
    queries, keys, values = lax.optimization_barrier(
        (dot_n(normed, w_q), dot_n(normed, w_k), dot_n(normed, w_v))
    )
    k_four = keys.reshape(seqs, rows, -1, HD)
    k_rot = k_four * cosine[:, None] + turn_plain(k_four) * sine[:, None]
    kv_own = jnp.concatenate(
        [k_rot.reshape(seqs, rows, kv_cols), values.reshape(seqs, rows, kv_cols)], -1
    ).astype(BF16)
    queries = queries.reshape(seqs, rows, -1)
    gain_own = lax.dynamic_slice_in_dim(gain, tensor_id * width_dev, width_dev, 0)
    x_mine = x_own.reshape(many, width_dev)
    rms_wide = jnp.broadcast_to(inv_rms, (many, HD))

    def backward(active, upstream_own, grad_q, grad_kv):
        return finish(
            n_tensor,
            active,
            grad_q.reshape(many, -1),
            grad_kv.reshape(many, -1),
            x_mine,
            upstream_own.reshape(many, width_dev),
            gain_own[None],
            rms_wide,
            w_q,
            w_k,
            w_v,
        )

    grad_q, grad_kv, kv_all = attend(
        n_tensor, 1, True, lengths, queries, place(resp_grad), kv_own, cosine, sine
    )
    first, first_low = backward(1, place(cotangent), grad_q, grad_kv)

    handed, grad_out = descend(n_tensor, first_low, w_o)
    grad_q, grad_kv = attend(
        n_tensor,
        0,
        False,
        lengths,
        queries,
        grad_out.reshape(seqs, rows, -1),
        kv_all,
        cosine,
        sine,
    )
    second, _ = backward(0, handed, grad_q, grad_kv)
    result = jnp.where(section_id == 0, second, first)
    return result.reshape(1, seqs, rows, width_dev)


def solution(mesh):
    return jax.shard_map(
        functools.partial(on_device, mesh.shape["tensor"]),
        mesh=mesh,
        in_specs=(
            P("section", None, "dp", "tensor"),
            P(None, None, "tensor"),
            P(),
            P(),
            P("section", None),
            P("section", None, "tensor"),
            P("section", None, "tensor"),
            P("section", None, "tensor"),
            P("section", "tensor", "dp"),
        ),
        out_specs=P("section", None, "dp", "tensor"),
        check_vma=False,
    )
```

```python
import functools
import math

import jax
import jax.numpy as jnp
from jax import lax
from jax.experimental import pallas as pl
from jax.experimental.pallas import tpu as pltpu
from jax.sharding import PartitionSpec as P

HD = 128
EPS = 1e-05
THETA = 500000.0
F32 = jnp.float32
BF16 = jnp.bfloat16


def dot_t(left, right):
    return lax.dot_general(left, right, (((1,), (1,)), ((), ())), preferred_element_type=F32)


def dot_n(left, right):
    return lax.dot_general(left, right, (((1,), (0,)), ((), ())), preferred_element_type=F32)


def dot_c(left, right):
    return lax.dot_general(left, right, (((0,), (0,)), ((), ())), preferred_element_type=F32)


def angle_tables(row_places):
    half_dim = HD // 2
    frequency = THETA ** (-(jnp.arange(half_dim, dtype=F32) * 2.0) / HD)
    angles = row_places[:, None] * frequency[None, :]
    cosine = jnp.concatenate([jnp.cos(angles), jnp.cos(angles)], -1)
    signed_sine = jnp.concatenate([-jnp.sin(angles), jnp.sin(angles)], -1)
    return cosine, signed_sine


def turn_plain(values):
    half_dim = HD // 2
    return jnp.concatenate([values[..., half_dim:], values[..., :half_dim]], -1)


MESH = pl.DeviceIdType.MESH
BIG = 56 * 1024 * 1024


def at(dp, section, tensor):
    return {"dp": dp, "section": section, "tensor": tensor}


def greet(where):
    pl.semaphore_signal(
        pltpu.get_barrier_semaphore(), inc=1, device_id=where, device_id_type=MESH
    )


def remote(src, dst, send_sem, recv_sem, where):
    return pltpu.make_async_remote_copy(
        src_ref=src,
        dst_ref=dst,
        send_sem=send_sem,
        recv_sem=recv_sem,
        device_id=where,
        device_id_type=MESH,
    )


def tiled_dot_t(left_ref, w_ref, store):
    tile = 256
    left = left_ref[...]

    def step(index, carry):
        start = pl.multiple_of(index * tile, tile)
        store(start, tile, dot_t(left, w_ref[pl.ds(start, tile), :]).astype(BF16))
        return carry

    lax.fori_loop(0, w_ref.shape[0] // tile, step, 0)


def opening_body(
    n, width, x_ref, cot_ref, w_ref, gain_ref, wq_ref, wk_ref, wv_ref,
    q_out, kv_out, rms_out, resp_out,
    x_box, cot_in, w_in, part, inbox, wq_in, wk_in, wv_in,
    x_send, x_recv, cot_sems, w_sem, part_send, part_recv, own_sem, tile_sems, turn_sem,
):
    d, sec, t = lax.axis_index("dp"), lax.axis_index("section"), lax.axis_index("tensor")
    many, wide = x_ref.shape
    kv_cols = wk_in.shape[2]
    deep = wq_in.shape[1]
    per = wide // deep
    crossing = jnp.where(d == t, 0, 1)
    onward = jnp.where(2 * t >= n, n - 1, 1)
    for k in range(1, n):
        greet(at(d, sec, lax.rem(t + k, n)))
        greet(at(lax.rem(d + k, n), sec, t))
    greet(at(d, 1 - sec, t))

    @pl.when(d != t)
    def _():
        greet(at(t, sec, d))

    pl.semaphore_wait(pltpu.get_barrier_semaphore(), 2 * n - 1 + crossing)

    own = pltpu.make_async_copy(x_ref, x_box.at[t], own_sem)
    own.start()

    def loads(count):
        owner = lax.rem(t + (count // per) * onward, n)
        rows = pl.ds(pl.multiple_of(owner * wide + lax.rem(count, per) * deep, deep), deep)
        slot = lax.rem(count, 2)
        return [
            pltpu.make_async_copy(source.at[rows, :], into.at[slot], tile_sems.at[slot, which])
            for which, (source, into) in enumerate(
                ((wq_ref, wq_in), (wk_ref, wk_in), (wv_ref, wv_in))
            )
        ]

    for load in loads(jnp.int32(0)):
        load.start()

    @pl.when(sec == 0)
    def _():
        pl.semaphore_wait(turn_sem, 1)

    def spread(k):
        return remote(
            x_ref, x_box.at[t], x_send.at[k], x_recv.at[t], at(d, sec, lax.rem(t + k, n))
        )

    for k in range(1, n):
        spread(k).start()

    w_load = pltpu.make_async_copy(w_ref, w_in, w_sem)
    swap = remote(cot_ref, cot_in, cot_sems.at[0], cot_sems.at[1], at(t, sec, d))
    keep = pltpu.make_async_copy(cot_ref, cot_in, cot_sems.at[2])

    @pl.when(sec == 1)
    def _():
        w_load.start()

        @pl.when(d != t)
        def _():
            swap.start()

        @pl.when(d == t)
        def _():
            keep.start()

    def give(k):
        return remote(
            part, inbox.at[d], part_send.at[k], part_recv.at[d], at(lax.rem(d + k, n), sec, t)
        )

    def respond():
        @pl.when(d != t)
        def _():
            swap.wait()

        @pl.when(d == t)
        def _():
            keep.wait()

        w_load.wait()

        def store(start, size, value):
            part[:, pl.ds(start, size)] = value

        tiled_dot_t(cot_in, w_in, store)
        for k in range(1, n):
            give(k).start()

    q_out[...] = jnp.zeros_like(q_out)
    kv_out[...] = jnp.zeros_like(kv_out)
    rms_out[...] = jnp.zeros_like(rms_out)
    own.wait()
    for step in range(n):
        owner = lax.rem(t + step * onward, n)
        if step:
            remote(
                x_ref, x_box.at[owner], x_send.at[step], x_recv.at[owner], at(d, sec, owner)
            ).wait_recv()
        if step == n - 1:

            @pl.when(sec == 1)
            def _():
                pl.semaphore_signal(
                    turn_sem, inc=1, device_id=at(d, 0, t), device_id_type=MESH
                )

        def project(index, carry):
            count = step * per + index

            @pl.when(count + 1 < n * per)
            def _():
                for load in loads(count + 1):
                    load.start()

            columns = pl.ds(pl.multiple_of(index * deep, deep), deep)
            piece = x_box[owner, :, columns].astype(F32)
            squares = jnp.sum(piece * piece, -1, keepdims=True)
            rms_out[...] += jnp.broadcast_to(squares, (many, HD))
            scaled = (piece * gain_ref[owner, :, columns]).astype(BF16)
            for load in loads(count):
                load.wait()
            slot = lax.rem(count, 2)
            q_out[...] += dot_n(scaled, wq_in[slot])
            kv_out[:, :kv_cols] += dot_n(scaled, wk_in[slot])
            kv_out[:, kv_cols:] += dot_n(scaled, wv_in[slot])
            return carry

        lax.fori_loop(0, per, project, 0)
        if step == 0:
            pl.when(sec == 1)(respond)

    tile = 16

    def settle(index, carry):
        rows = pl.ds(pl.multiple_of(index * tile, tile), tile)
        rms = lax.rsqrt(rms_out[rows, :] / width + EPS)
        rms_out[rows, :] = rms
        q_out[rows, :] = q_out[rows, :] * rms[:, :1]
        kv_out[rows, :] = kv_out[rows, :] * rms[:, :1]
        return carry

    lax.fori_loop(0, many // tile, settle, 0)

    @pl.when(sec == 1)
    def _():
        total = part[...].astype(F32)
        for k in range(1, n):
            peer = lax.rem(d + k, n)
            remote(
                part, inbox.at[peer], part_send.at[k], part_recv.at[peer], at(peer, sec, t)
            ).wait_recv()
            total = total + inbox[peer].astype(F32)
        resp_out[...] = total.astype(BF16)
        for k in range(1, n):
            give(k).wait_send()

    for k in range(1, n):
        spread(k).wait_send()


def opening(n, x, cot, w, gain, wq, wk, wv):
    many, wide = x.shape
    resp = cot.shape[0]
    cols = w.shape[0]
    kv_cols = wk.shape[1]
    deep = 512
    dma = pltpu.SemaphoreType.DMA
    vmem = pl.BlockSpec(memory_space=pltpu.VMEM)
    hbm = pl.BlockSpec(memory_space=pl.ANY)
    return pl.pallas_call(
        functools.partial(opening_body, n, wq.shape[0]),
        in_specs=[hbm, hbm, hbm, vmem, hbm, hbm, hbm],
        out_specs=[vmem] * 4,
        out_shape=[
            jax.ShapeDtypeStruct((many, cols), F32),
            jax.ShapeDtypeStruct((many, 2 * kv_cols), F32),
            jax.ShapeDtypeStruct((many, HD), F32),
            jax.ShapeDtypeStruct((resp, cols), BF16),
        ],
        scratch_shapes=[
            pltpu.VMEM((n, many, wide), BF16),
            pltpu.VMEM((resp, wide), BF16),
            pltpu.VMEM(w.shape, BF16),
            pltpu.VMEM((resp, cols), BF16),
            pltpu.VMEM((n, resp, cols), BF16),
            pltpu.VMEM((2, deep, cols), BF16),
            pltpu.VMEM((2, deep, kv_cols), BF16),
            pltpu.VMEM((2, deep, kv_cols), BF16),
            dma((n,)),
            dma((n,)),
            dma((3,)),
            dma,
            dma((n,)),
            dma((n,)),
            dma,
            dma((2, 3)),
            pltpu.SemaphoreType.REGULAR,
        ],
        compiler_params=pltpu.CompilerParams(
            collective_id=0, has_side_effects=True, vmem_limit_bytes=BIG
        ),
    )(x, cot, w, gain.reshape(n, 1, wide), wq, wk, wv)


def finish_body(
    n, active, width, gq_ref, gkv_ref, x_ref, up_ref, gain_ref, rms_ref, wq_ref, wk_ref, wv_ref,
    out_ref, low_ref, inbox, outbox, stats, wq_in, wk_in, wv_in, w_sems,
    send, recv, stat_send, stat_recv,
):
    d, sec, t = lax.axis_index("dp"), lax.axis_index("section"), lax.axis_index("tensor")
    many, wide = x_ref.shape
    kv_cols = wk_in.shape[2]
    tile = 16
    deep = wq_in.shape[1]
    per = wide // deep

    for k in range(1, n):
        greet(at(d, sec, lax.rem(t + k, n)))
    pl.semaphore_wait(pltpu.get_barrier_semaphore(), n - 1)

    @pl.when(sec == active)
    def _():
        def loads(count):
            owner = lax.rem(t + 1 + count // per, n)
            rows = pl.ds(pl.multiple_of(owner * wide + lax.rem(count, per) * deep, deep), deep)
            slot = lax.rem(count, 2)
            return [
                pltpu.make_async_copy(source.at[rows, :], into.at[slot], w_sems.at[slot, which])
                for which, (source, into) in enumerate(
                    ((wq_ref, wq_in), (wk_ref, wk_in), (wv_ref, wv_in))
                )
            ]

        def push(k, index):
            peer = lax.rem(t + k, n)
            columns = pl.ds(pl.multiple_of(index * deep, deep), deep)
            return remote(
                outbox.at[peer, :, columns],
                inbox.at[t, :, columns],
                send.at[k, index],
                recv.at[t, index],
                at(d, sec, peer),
            )

        for load in loads(jnp.int32(0)):
            load.start()
        for k in range(1, n + 1):
            owner = lax.rem(t + k, n)

            def project(index, carry):
                count = (k - 1) * per + index

                @pl.when(count + 1 < n * per)
                def _():
                    for load in loads(count + 1):
                        load.start()

                for load in loads(count):
                    load.wait()
                slot = lax.rem(count, 2)
                value = (
                    dot_t(gq_ref[...], wq_in[slot])
                    + dot_t(gkv_ref[:, :kv_cols], wk_in[slot])
                    + dot_t(gkv_ref[:, kv_cols:], wv_in[slot])
                ).astype(BF16)
                columns = pl.ds(pl.multiple_of(index * deep, deep), deep)
                if k < n:
                    outbox[owner, :, columns] = value
                    push(k, index).start()
                else:
                    inbox[owner, :, columns] = value
                return carry

            lax.fori_loop(0, per, project, 0)

        for k in range(1, n):
            peer = lax.rem(t + k, n)
            for index in range(per):
                columns = pl.ds(index * deep, deep)
                remote(
                    outbox.at[peer, :, columns],
                    inbox.at[peer, :, columns],
                    send.at[k, index],
                    recv.at[peer, index],
                    at(d, sec, peer),
                ).wait_recv()

        def gather_sum(index, carry):
            rows = pl.ds(pl.multiple_of(index * tile, tile), tile)
            total = inbox[0, rows, :].astype(F32)
            for j in range(1, n):
                total = total + inbox[j, rows, :].astype(F32)
            scaled = total * gain_ref[...]
            out_ref[rows, :] = scaled
            dots = jnp.sum(x_ref[rows, :].astype(F32) * scaled, -1, keepdims=True)
            stats[t, rows, :] = jnp.broadcast_to(dots, (tile, HD))
            return carry

        lax.fori_loop(0, many // tile, gather_sum, 0)

        for k in range(1, n):
            peer = lax.rem(t + k, n)
            remote(
                stats.at[t], stats.at[t], stat_send.at[k], stat_recv.at[t], at(d, sec, peer)
            ).start()
        for k in range(1, n):
            peer = lax.rem(t + k, n)
            remote(
                stats.at[peer], stats.at[peer], stat_send.at[k], stat_recv.at[peer],
                at(d, sec, peer),
            ).wait_recv()

        def settle(index, carry):
            rows = pl.ds(pl.multiple_of(index * tile, tile), tile)
            stat = stats[0, rows, :]
            for j in range(1, n):
                stat = stat + stats[j, rows, :]
            rms = rms_ref[rows, :]
            factor = (rms * rms * rms * stat / width)[:, :1]
            value = (
                up_ref[rows, :].astype(F32)
                + rms[:, :1] * out_ref[rows, :]
                - x_ref[rows, :].astype(F32) * factor
            )
            out_ref[rows, :] = value
            low_ref[rows, :] = value.astype(BF16)
            return carry

        lax.fori_loop(0, many // tile, settle, 0)
        for k in range(1, n):
            for index in range(per):
                push(k, index).wait_send()
            peer = lax.rem(t + k, n)
            remote(
                stats.at[t], stats.at[t], stat_send.at[k], stat_recv.at[t], at(d, sec, peer)
            ).wait_send()


def finish(n, active, gq, gkv, x, up, gain, rms, wq, wk, wv):
    many, wide = x.shape
    deep = 512
    dma = pltpu.SemaphoreType.DMA
    vmem = pl.BlockSpec(memory_space=pltpu.VMEM)
    return pl.pallas_call(
        functools.partial(finish_body, n, active, wq.shape[0]),
        in_specs=[vmem] * 6 + [pl.BlockSpec(memory_space=pl.ANY)] * 3,
        out_specs=[vmem, vmem],
        out_shape=[
            jax.ShapeDtypeStruct((many, wide), F32),
            jax.ShapeDtypeStruct((many, wide), BF16),
        ],
        scratch_shapes=[
            pltpu.VMEM((n, many, wide), BF16),
            pltpu.VMEM((n, many, wide), BF16),
            pltpu.VMEM((n, many, HD), F32),
            pltpu.VMEM((2, deep, wq.shape[1]), BF16),
            pltpu.VMEM((2, deep, wk.shape[1]), BF16),
            pltpu.VMEM((2, deep, wv.shape[1]), BF16),
            dma((2, 3)),
            dma((n, wide // deep)),
            dma((n, wide // deep)),
            dma((n,)),
            dma((n,)),
        ],
        compiler_params=pltpu.CompilerParams(
            collective_id=1 + active, has_side_effects=True, vmem_limit_bytes=BIG
        ),
    )(gq, gkv, x, up, gain, rms, wq, wk, wv)


def descend_body(
    n, g_ref, w_ref, up_out, go_out, mid, spread, w_in, outbox, inbox,
    g_send, g_recv, s_send, s_recv, p_send, p_recv, w_sem, up_sem,
):
    d, sec, t = lax.axis_index("dp"), lax.axis_index("section"), lax.axis_index("tensor")
    for k in range(n):
        greet(at(d, 1 - sec, lax.rem(t + k, n)))

    @pl.when(sec == 0)
    def _():
        for k in range(1, n):
            greet(at(lax.rem(d + k, n), sec, t))

    pl.semaphore_wait(pltpu.get_barrier_semaphore(), n + (1 - sec) * (n - 1))

    def hand(k):
        return remote(
            g_ref, mid.at[t], g_send.at[k], g_recv.at[t], at(d, 0, lax.rem(t + k, n))
        )

    @pl.when(sec == 1)
    def _():
        for k in range(n):
            hand(k).start()
        for k in range(n):
            hand(k).wait_send()

    @pl.when(sec == 0)
    def _():
        load = pltpu.make_async_copy(w_ref, w_in, w_sem)
        load.start()

        def arrived(slot):
            remote(
                mid.at[slot], mid.at[slot], g_send.at[0], g_recv.at[slot], at(d, 1, slot)
            ).wait_recv()

        def move(k):
            peer = lax.rem(d + k, n)
            return remote(
                mid.at[peer], spread.at[d], s_send.at[k], s_recv.at[d], at(peer, 0, t)
            )

        for k in range(1, n):
            arrived(lax.rem(d + k, n))
            move(k).start()
        arrived(d)
        keep = pltpu.make_async_copy(mid.at[t], up_out, up_sem)
        keep.start()
        load.wait()

        def give(k):
            peer = lax.rem(d + k, n)
            return remote(
                outbox.at[peer], inbox.at[d], p_send.at[k], p_recv.at[d], at(peer, 0, t)
            )

        for k in range(1, n):
            peer = lax.rem(d + k, n)
            remote(
                spread.at[peer], spread.at[peer], s_send.at[k], s_recv.at[peer],
                at(peer, 0, t),
            ).wait_recv()

            def store(start, size, value):
                outbox[peer, :, pl.ds(start, size)] = value

            tiled_dot_t(spread.at[peer], w_in, store)
            give(k).start()

        def store_own(start, size, value):
            outbox[d, :, pl.ds(start, size)] = value

        tiled_dot_t(mid.at[d], w_in, store_own)
        for k in range(1, n):
            peer = lax.rem(d + k, n)
            remote(
                inbox.at[peer], inbox.at[peer], p_send.at[k], p_recv.at[peer],
                at(peer, 0, t),
            ).wait_recv()
        tile = 16

        def add(index, carry):
            rows = pl.ds(pl.multiple_of(index * tile, tile), tile)
            total = outbox[d, rows, :].astype(F32)
            for k in range(1, n):
                total = total + inbox[lax.rem(d + k, n), rows, :].astype(F32)
            go_out[rows, :] = total.astype(BF16)
            return carry

        lax.fori_loop(0, go_out.shape[0] // tile, add, 0)
        keep.wait()
        for k in range(1, n):
            move(k).wait_send()
            give(k).wait_send()


def descend(n, g, w):
    many, wide = g.shape
    cols = w.shape[0]
    dma = pltpu.SemaphoreType.DMA
    vmem = pl.BlockSpec(memory_space=pltpu.VMEM)
    return pl.pallas_call(
        functools.partial(descend_body, n),
        in_specs=[vmem, pl.BlockSpec(memory_space=pl.ANY)],
        out_specs=[vmem, vmem],
        out_shape=[
            jax.ShapeDtypeStruct((many, wide), BF16),
            jax.ShapeDtypeStruct((many, cols), BF16),
        ],
        scratch_shapes=[
            pltpu.VMEM((n, many, wide), BF16),
            pltpu.VMEM((n, many, wide), BF16),
            pltpu.VMEM(w.shape, BF16),
            pltpu.VMEM((n, many, cols), BF16),
            pltpu.VMEM((n, many, cols), BF16),
            dma((n,)),
            dma((n,)),
            dma((n,)),
            dma((n,)),
            dma((n,)),
            dma((n,)),
            dma,
            dma,
        ],
        compiler_params=pltpu.CompilerParams(
            collective_id=3, has_side_effects=True, vmem_limit_bytes=BIG
        ),
    )(g, w)


def attend_body(n, active, gather, lens_ref, q_ref, o_ref, kv_ref, cos_ref, sin_ref, *rest):
    if gather:
        gq_ref, gkv_ref, kv_out, kv_box, terms, inbox, kv_send, kv_recv, send, recv = rest
    else:
        gq_ref, gkv_ref, terms, inbox, send, recv = rest
        kv_box = kv_ref
    d, sec, t = lax.axis_index("dp"), lax.axis_index("section"), lax.axis_index("tensor")
    batch, rows, cols = q_ref.shape
    kv_cols = kv_box.shape[3] // 2
    kv_dev = kv_cols // HD
    group = cols // kv_cols
    length = n * rows
    many = rows * group
    scale = 1.0 / math.sqrt(HD)
    for k in range(1, n):
        greet(at(lax.rem(d + k, n), sec, t))
    pl.semaphore_wait(pltpu.get_barrier_semaphore(), n - 1)

    if gather:
        for k in range(1, n):
            remote(
                kv_ref, kv_box.at[d], kv_send.at[k], kv_recv.at[d],
                at(lax.rem(d + k, n), sec, t),
            ).start()
        kv_box[d] = kv_ref[...]
        for k in range(1, n):
            peer = lax.rem(d + k, n)
            remote(
                kv_ref, kv_box.at[peer], kv_send.at[k], kv_recv.at[peer], at(peer, sec, t)
            ).wait_recv()
        kv_out[...] = kv_box[...]

    @pl.when(sec == active)
    def _():
        cosine, sine = cos_ref[...], sin_ref[...]

        def one(index, carry):
            seq = index // kv_dev
            kv_head = lax.rem(index, kv_dev)
            k_lanes = pl.ds(pl.multiple_of(kv_head * HD, HD), HD)
            v_lanes = pl.ds(pl.multiple_of(kv_cols + kv_head * HD, HD), HD)

            def q_lanes(head):
                return pl.ds(pl.multiple_of((kv_head * group + head) * HD, HD), HD)

            q_parts, o_parts = [], []
            for head in range(group):
                raw = q_ref[seq, :, q_lanes(head)]
                turned = raw * cosine + pltpu.roll(raw, HD // 2, 1) * sine
                q_parts.append(turned.astype(BF16))
                o_parts.append(o_ref[seq, :, q_lanes(head)])
            q_all = jnp.concatenate(q_parts, 0)
            o_all = jnp.concatenate(o_parts, 0)
            keys = jnp.concatenate([kv_box[r, seq, :, k_lanes] for r in range(n)], 0)
            values = jnp.concatenate([kv_box[r, seq, :, v_lanes] for r in range(n)], 0)
            row_at = lax.broadcasted_iota(jnp.int32, (many, length), 0) & (rows - 1)
            query_at = d * rows + row_at
            key_at = lax.broadcasted_iota(jnp.int32, (many, length), 1)
            start = length - lens_ref[seq]
            allowed = (key_at == query_at) | ((key_at < query_at) & (key_at >= start))
            scores = jnp.where(allowed, dot_t(q_all, keys) * scale, -1e30)
            highest = jnp.max(scores, -1, keepdims=True)
            terms_e = jnp.where(allowed, jnp.exp(scores - highest), 0.0)
            probs = terms_e / jnp.sum(terms_e, -1, keepdims=True)
            grad_probs = dot_t(o_all, values)
            row_dot = jnp.sum(probs * grad_probs, -1, keepdims=True)
            grad_scores = (probs * (grad_probs - row_dot) * scale).astype(BF16)
            grad_qr = dot_n(grad_scores, keys)
            grad_k = dot_c(grad_scores, q_all).astype(BF16)
            grad_v = dot_c(probs.astype(BF16), o_all).astype(BF16)
            for r in range(n):
                terms[r, seq, :, k_lanes] = grad_k[r * rows : (r + 1) * rows]
                terms[r, seq, :, v_lanes] = grad_v[r * rows : (r + 1) * rows]
            for head in range(group):
                part = grad_qr[head * rows : (head + 1) * rows]
                turned = part * cosine - pltpu.roll(part, HD // 2, 1) * sine
                gq_ref[seq, :, q_lanes(head)] = turned.astype(BF16)
            return carry

        lax.fori_loop(0, batch * kv_dev, one, 0)

        def push(k):
            peer = lax.rem(d + k, n)
            return remote(
                terms.at[peer], inbox.at[d], send.at[k], recv.at[d], at(peer, sec, t)
            )

        for k in range(1, n):
            push(k).start()
        inbox[d] = terms[d]
        for k in range(1, n):
            peer = lax.rem(d + k, n)
            remote(
                terms.at[peer], inbox.at[peer], send.at[k], recv.at[peer], at(peer, sec, t)
            ).wait_recv()
        for seq in range(batch):
            total = inbox[0, seq].astype(F32)
            for r in range(1, n):
                total = total + inbox[r, seq].astype(F32)
            for head in range(kv_dev):
                lanes = slice(head * HD, (head + 1) * HD)
                part = total[:, lanes]
                turned = part * cosine - pltpu.roll(part, HD // 2, 1) * sine
                gkv_ref[seq, :, lanes] = turned.astype(BF16)
            gkv_ref[seq, :, kv_cols:] = total[:, kv_cols:].astype(BF16)
        for k in range(1, n):
            push(k).wait_send()

    if gather:
        for k in range(1, n):
            remote(
                kv_ref, kv_box.at[d], kv_send.at[k], kv_recv.at[d],
                at(lax.rem(d + k, n), sec, t),
            ).wait_send()


def attend(n, active, gather, lengths, queries, grad_out, kv, cosine, sine):
    batch, rows, cols = queries.shape
    both = kv.shape[-1]
    dma = pltpu.SemaphoreType.DMA
    vmem = pl.BlockSpec(memory_space=pltpu.VMEM)
    whole = (n, batch, rows, both)
    out_shape = [
        jax.ShapeDtypeStruct((batch, rows, cols), BF16),
        jax.ShapeDtypeStruct((batch, rows, both), BF16),
    ]
    scratch = [pltpu.VMEM(whole, BF16), pltpu.VMEM(whole, BF16)]
    sems = [dma((n,)), dma((n,))]
    if gather:
        out_shape.append(jax.ShapeDtypeStruct(whole, BF16))
        scratch.append(pltpu.VMEM(whole, BF16))
        sems = sems + sems
    return pl.pallas_call(
        functools.partial(attend_body, n, active, gather),
        in_specs=[pl.BlockSpec(memory_space=pltpu.SMEM)] + [vmem] * 5,
        out_specs=[vmem] * len(out_shape),
        out_shape=out_shape,
        scratch_shapes=scratch + sems,
        compiler_params=pltpu.CompilerParams(
            collective_id=4 + active, has_side_effects=True, vmem_limit_bytes=BIG
        ),
    )(lengths, queries, grad_out, kv, cosine, sine)


def on_device(
    n_tensor, stored, cotangent, positions, lengths, norm_gain, w_query, w_key, w_value, w_out
):
    x_own = stored[0]
    gain = norm_gain[0]
    w_q, w_k, w_v, w_o = w_query[0], w_key[0], w_value[0], w_out[0]
    seqs, rows, width_dev = x_own.shape
    many = seqs * rows
    width = gain.shape[0]
    kv_cols = w_k.shape[1]
    dp_id = lax.axis_index("dp")
    tensor_id = lax.axis_index("tensor")
    section_id = lax.axis_index("section")
    row_ids = dp_id * rows + jnp.arange(rows, dtype=jnp.int32)
    cosine, sine = angle_tables(row_ids.astype(F32))
    resp = cotangent.shape[1]
    queries, key_values, rms_wide, resp_grad = opening(
        n_tensor,
        x_own.reshape(many, width_dev),
        cotangent.reshape(seqs * resp, width_dev),
        w_o,
        gain,
        w_q,
        w_k,
        w_v,
    )
    resp_grad = resp_grad.reshape(seqs, resp, -1)
    placed = (positions[:, None, :] == row_ids[None, :, None]).astype(BF16)

    def place(small):
        return jnp.einsum("spr,srd->spd", placed, small, preferred_element_type=F32).astype(BF16)

    keys, values = key_values[:, :kv_cols], key_values[:, kv_cols:]
    k_four = keys.reshape(seqs, rows, -1, HD)
    k_rot = k_four * cosine[:, None] + turn_plain(k_four) * sine[:, None]
    kv_own = jnp.concatenate(
        [k_rot.reshape(seqs, rows, kv_cols), values.reshape(seqs, rows, kv_cols)], -1
    ).astype(BF16)
    queries = queries.reshape(seqs, rows, -1)
    gain_own = lax.dynamic_slice_in_dim(gain, tensor_id * width_dev, width_dev, 0)
    x_mine = x_own.reshape(many, width_dev)

    def backward(active, upstream_own, grad_q, grad_kv):
        return finish(
            n_tensor,
            active,
            grad_q.reshape(many, -1),
            grad_kv.reshape(many, -1),
            x_mine,
            upstream_own.reshape(many, width_dev),
            gain_own[None],
            rms_wide,
            w_q,
            w_k,
            w_v,
        )

    grad_q, grad_kv, kv_all = attend(
        n_tensor, 1, True, lengths, queries, place(resp_grad), kv_own, cosine, sine
    )
    first, first_low = backward(1, place(cotangent), grad_q, grad_kv)

    handed, grad_out = descend(n_tensor, first_low, w_o)
    grad_q, grad_kv = attend(
        n_tensor,
        0,
        False,
        lengths,
        queries,
        grad_out.reshape(seqs, rows, -1),
        kv_all,
        cosine,
        sine,
    )
    second, _ = backward(0, handed, grad_q, grad_kv)
    result = jnp.where(section_id == 0, second, first)
    return result.reshape(1, seqs, rows, width_dev)


def solution(mesh):
    return jax.shard_map(
        functools.partial(on_device, mesh.shape["tensor"]),
        mesh=mesh,
        in_specs=(
            P("section", None, "dp", "tensor"),
            P(None, None, "tensor"),
            P(),
            P(),
            P("section", None),
            P("section", None, "tensor"),
            P("section", None, "tensor"),
            P("section", None, "tensor"),
            P("section", "tensor", "dp"),
        ),
        out_specs=P("section", None, "dp", "tensor"),
        check_vma=False,
    )
```

```python
import functools
import math

import jax
import jax.numpy as jnp
from jax import lax
from jax.experimental import pallas as pl
from jax.experimental.pallas import tpu as pltpu
from jax.sharding import PartitionSpec as P

HD = 128
EPS = 1e-05
THETA = 500000.0
F32 = jnp.float32
BF16 = jnp.bfloat16


def dot_t(left, right):
    return lax.dot_general(left, right, (((1,), (1,)), ((), ())), preferred_element_type=F32)


def dot_n(left, right):
    return lax.dot_general(left, right, (((1,), (0,)), ((), ())), preferred_element_type=F32)


def dot_c(left, right):
    return lax.dot_general(left, right, (((0,), (0,)), ((), ())), preferred_element_type=F32)


def angle_tables(row_places):
    half_dim = HD // 2
    frequency = THETA ** (-(jnp.arange(half_dim, dtype=F32) * 2.0) / HD)
    angles = row_places[:, None] * frequency[None, :]
    cosine = jnp.concatenate([jnp.cos(angles), jnp.cos(angles)], -1)
    signed_sine = jnp.concatenate([-jnp.sin(angles), jnp.sin(angles)], -1)
    return cosine, signed_sine


def turn_plain(values):
    half_dim = HD // 2
    return jnp.concatenate([values[..., half_dim:], values[..., :half_dim]], -1)


MESH = pl.DeviceIdType.MESH
BIG = 56 * 1024 * 1024


def at(dp, section, tensor):
    return {"dp": dp, "section": section, "tensor": tensor}


def greet(where):
    pl.semaphore_signal(
        pltpu.get_barrier_semaphore(), inc=1, device_id=where, device_id_type=MESH
    )


def remote(src, dst, send_sem, recv_sem, where):
    return pltpu.make_async_remote_copy(
        src_ref=src,
        dst_ref=dst,
        send_sem=send_sem,
        recv_sem=recv_sem,
        device_id=where,
        device_id_type=MESH,
    )


def tiled_dot_t(left_ref, w_ref, store):
    tile = 256
    left = left_ref[...]

    def step(index, carry):
        start = pl.multiple_of(index * tile, tile)
        store(start, tile, dot_t(left, w_ref[pl.ds(start, tile), :]).astype(BF16))
        return carry

    lax.fori_loop(0, w_ref.shape[0] // tile, step, 0)


def opening_body(
    n, width, x_ref, cot_ref, w_ref, gain_ref, wq_ref, wk_ref, wv_ref,
    q_out, kv_out, rms_out, resp_out,
    x_box, cot_in, w_in, part, inbox, wq_in, wk_in, wv_in,
    x_send, x_recv, cot_sems, w_sem, part_send, part_recv, own_sem, tile_sems, turn_sem,
):
    d, sec, t = lax.axis_index("dp"), lax.axis_index("section"), lax.axis_index("tensor")
    many, wide = x_ref.shape
    kv_cols = wk_in.shape[2]
    deep = wq_in.shape[1]
    per = wide // deep
    crossing = jnp.where(d == t, 0, 1)
    onward = jnp.where(2 * t >= n, n - 1, 1)
    for k in range(1, n):
        greet(at(d, sec, lax.rem(t + k, n)))
        greet(at(lax.rem(d + k, n), sec, t))
    greet(at(d, 1 - sec, t))

    @pl.when(d != t)
    def _():
        greet(at(t, sec, d))

    pl.semaphore_wait(pltpu.get_barrier_semaphore(), 2 * n - 1 + crossing)

    own = pltpu.make_async_copy(x_ref, x_box.at[t], own_sem)
    own.start()

    def loads(count):
        owner = lax.rem(t + (count // per) * onward, n)
        rows = pl.ds(pl.multiple_of(owner * wide + lax.rem(count, per) * deep, deep), deep)
        slot = lax.rem(count, 2)
        return [
            pltpu.make_async_copy(source.at[rows, :], into.at[slot], tile_sems.at[slot, which])
            for which, (source, into) in enumerate(
                ((wq_ref, wq_in), (wk_ref, wk_in), (wv_ref, wv_in))
            )
        ]

    for load in loads(jnp.int32(0)):
        load.start()

    @pl.when(sec == 0)
    def _():
        pl.semaphore_wait(turn_sem, 1)

    def spread(k):
        return remote(
            x_ref, x_box.at[t], x_send.at[k], x_recv.at[t], at(d, sec, lax.rem(t + k, n))
        )

    for k in range(1, n):
        spread(k).start()

    w_load = pltpu.make_async_copy(w_ref, w_in, w_sem)
    swap = remote(cot_ref, cot_in, cot_sems.at[0], cot_sems.at[1], at(t, sec, d))
    keep = pltpu.make_async_copy(cot_ref, cot_in, cot_sems.at[2])

    @pl.when(sec == 1)
    def _():
        w_load.start()

        @pl.when(d != t)
        def _():
            swap.start()

        @pl.when(d == t)
        def _():
            keep.start()

    def give(k):
        return remote(
            part, inbox.at[d], part_send.at[k], part_recv.at[d], at(lax.rem(d + k, n), sec, t)
        )

    def respond():
        @pl.when(d != t)
        def _():
            swap.wait()

        @pl.when(d == t)
        def _():
            keep.wait()

        w_load.wait()

        def store(start, size, value):
            part[:, pl.ds(start, size)] = value

        tiled_dot_t(cot_in, w_in, store)
        for k in range(1, n):
            give(k).start()

    q_out[...] = jnp.zeros_like(q_out)
    kv_out[...] = jnp.zeros_like(kv_out)
    rms_out[...] = jnp.zeros_like(rms_out)
    own.wait()
    for step in range(n):
        owner = lax.rem(t + step * onward, n)
        if step:
            remote(
                x_ref, x_box.at[owner], x_send.at[step], x_recv.at[owner], at(d, sec, owner)
            ).wait_recv()
        if step == n - 1:

            @pl.when(sec == 1)
            def _():
                pl.semaphore_signal(
                    turn_sem, inc=1, device_id=at(d, 0, t), device_id_type=MESH
                )

        def project(index, carry):
            count = step * per + index

            @pl.when(count + 1 < n * per)
            def _():
                for load in loads(count + 1):
                    load.start()

            columns = pl.ds(pl.multiple_of(index * deep, deep), deep)
            piece = x_box[owner, :, columns].astype(F32)
            squares = jnp.sum(piece * piece, -1, keepdims=True)
            rms_out[...] += jnp.broadcast_to(squares, (many, HD))
            scaled = (piece * gain_ref[owner, :, columns]).astype(BF16)
            for load in loads(count):
                load.wait()
            slot = lax.rem(count, 2)
            q_out[...] += dot_n(scaled, wq_in[slot])
            kv_out[:, :kv_cols] += dot_n(scaled, wk_in[slot])
            kv_out[:, kv_cols:] += dot_n(scaled, wv_in[slot])
            return carry

        lax.fori_loop(0, per, project, 0)
        if step == 0:
            pl.when(sec == 1)(respond)

    tile = 16

    def settle(index, carry):
        rows = pl.ds(pl.multiple_of(index * tile, tile), tile)
        rms = lax.rsqrt(rms_out[rows, :] / width + EPS)
        rms_out[rows, :] = rms
        q_out[rows, :] = q_out[rows, :] * rms[:, :1]
        kv_out[rows, :] = kv_out[rows, :] * rms[:, :1]
        return carry

    lax.fori_loop(0, many // tile, settle, 0)

    @pl.when(sec == 1)
    def _():
        total = part[...].astype(F32)
        for k in range(1, n):
            peer = lax.rem(d + k, n)
            remote(
                part, inbox.at[peer], part_send.at[k], part_recv.at[peer], at(peer, sec, t)
            ).wait_recv()
            total = total + inbox[peer].astype(F32)
        resp_out[...] = total.astype(BF16)
        for k in range(1, n):
            give(k).wait_send()

    for k in range(1, n):
        spread(k).wait_send()


def opening(n, x, cot, w, gain, wq, wk, wv):
    many, wide = x.shape
    resp = cot.shape[0]
    cols = w.shape[0]
    kv_cols = wk.shape[1]
    deep = 512
    dma = pltpu.SemaphoreType.DMA
    vmem = pl.BlockSpec(memory_space=pltpu.VMEM)
    hbm = pl.BlockSpec(memory_space=pl.ANY)
    return pl.pallas_call(
        functools.partial(opening_body, n, wq.shape[0]),
        in_specs=[hbm, hbm, hbm, vmem, hbm, hbm, hbm],
        out_specs=[vmem] * 4,
        out_shape=[
            jax.ShapeDtypeStruct((many, cols), F32),
            jax.ShapeDtypeStruct((many, 2 * kv_cols), F32),
            jax.ShapeDtypeStruct((many, HD), F32),
            jax.ShapeDtypeStruct((resp, cols), BF16),
        ],
        scratch_shapes=[
            pltpu.VMEM((n, many, wide), BF16),
            pltpu.VMEM((resp, wide), BF16),
            pltpu.VMEM(w.shape, BF16),
            pltpu.VMEM((resp, cols), BF16),
            pltpu.VMEM((n, resp, cols), BF16),
            pltpu.VMEM((2, deep, cols), BF16),
            pltpu.VMEM((2, deep, kv_cols), BF16),
            pltpu.VMEM((2, deep, kv_cols), BF16),
            dma((n,)),
            dma((n,)),
            dma((3,)),
            dma,
            dma((n,)),
            dma((n,)),
            dma,
            dma((2, 3)),
            pltpu.SemaphoreType.REGULAR,
        ],
        compiler_params=pltpu.CompilerParams(
            collective_id=0, has_side_effects=True, vmem_limit_bytes=BIG
        ),
    )(x, cot, w, gain.reshape(n, 1, wide), wq, wk, wv)


def finish_body(
    n, active, width, gq_ref, gkv_ref, x_ref, up_ref, gain_ref, rms_ref, wq_ref, wk_ref, wv_ref,
    out_ref, low_ref, inbox, outbox, stats, wq_in, wk_in, wv_in, w_sems,
    send, recv, stat_send, stat_recv,
):
    d, sec, t = lax.axis_index("dp"), lax.axis_index("section"), lax.axis_index("tensor")
    many, wide = x_ref.shape
    kv_cols = wk_in.shape[2]
    tile = 16
    deep = wq_in.shape[1]
    per = wide // deep

    for k in range(1, n):
        greet(at(d, sec, lax.rem(t + k, n)))
    pl.semaphore_wait(pltpu.get_barrier_semaphore(), n - 1)

    @pl.when(sec == active)
    def _():
        def loads(count):
            owner = lax.rem(t + 1 + count // per, n)
            rows = pl.ds(pl.multiple_of(owner * wide + lax.rem(count, per) * deep, deep), deep)
            slot = lax.rem(count, 2)
            return [
                pltpu.make_async_copy(source.at[rows, :], into.at[slot], w_sems.at[slot, which])
                for which, (source, into) in enumerate(
                    ((wq_ref, wq_in), (wk_ref, wk_in), (wv_ref, wv_in))
                )
            ]

        def push(k, index):
            peer = lax.rem(t + k, n)
            columns = pl.ds(pl.multiple_of(index * deep, deep), deep)
            return remote(
                outbox.at[peer, :, columns],
                inbox.at[t, :, columns],
                send.at[k, index],
                recv.at[t, index],
                at(d, sec, peer),
            )

        for load in loads(jnp.int32(0)):
            load.start()
        for k in range(1, n + 1):
            owner = lax.rem(t + k, n)

            def project(index, carry):
                count = (k - 1) * per + index

                @pl.when(count + 1 < n * per)
                def _():
                    for load in loads(count + 1):
                        load.start()

                for load in loads(count):
                    load.wait()
                slot = lax.rem(count, 2)
                value = (
                    dot_t(gq_ref[...], wq_in[slot])
                    + dot_t(gkv_ref[:, :kv_cols], wk_in[slot])
                    + dot_t(gkv_ref[:, kv_cols:], wv_in[slot])
                ).astype(BF16)
                columns = pl.ds(pl.multiple_of(index * deep, deep), deep)
                if k < n:
                    outbox[owner, :, columns] = value
                    push(k, index).start()
                else:
                    inbox[owner, :, columns] = value
                return carry

            lax.fori_loop(0, per, project, 0)

        for k in range(1, n):
            peer = lax.rem(t + k, n)
            for index in range(per):
                columns = pl.ds(index * deep, deep)
                remote(
                    outbox.at[peer, :, columns],
                    inbox.at[peer, :, columns],
                    send.at[k, index],
                    recv.at[peer, index],
                    at(d, sec, peer),
                ).wait_recv()

        def gather_sum(index, carry):
            rows = pl.ds(pl.multiple_of(index * tile, tile), tile)
            total = inbox[0, rows, :].astype(F32)
            for j in range(1, n):
                total = total + inbox[j, rows, :].astype(F32)
            scaled = total * gain_ref[...]
            out_ref[rows, :] = scaled
            dots = jnp.sum(x_ref[rows, :].astype(F32) * scaled, -1, keepdims=True)
            stats[t, rows, :] = jnp.broadcast_to(dots, (tile, HD))
            return carry

        lax.fori_loop(0, many // tile, gather_sum, 0)

        for k in range(1, n):
            peer = lax.rem(t + k, n)
            remote(
                stats.at[t], stats.at[t], stat_send.at[k], stat_recv.at[t], at(d, sec, peer)
            ).start()
        for k in range(1, n):
            peer = lax.rem(t + k, n)
            remote(
                stats.at[peer], stats.at[peer], stat_send.at[k], stat_recv.at[peer],
                at(d, sec, peer),
            ).wait_recv()

        def settle(index, carry):
            rows = pl.ds(pl.multiple_of(index * tile, tile), tile)
            stat = stats[0, rows, :]
            for j in range(1, n):
                stat = stat + stats[j, rows, :]
            rms = rms_ref[rows, :]
            factor = (rms * rms * rms * stat / width)[:, :1]
            value = (
                up_ref[rows, :].astype(F32)
                + rms[:, :1] * out_ref[rows, :]
                - x_ref[rows, :].astype(F32) * factor
            )
            out_ref[rows, :] = value
            low_ref[rows, :] = value.astype(BF16)
            return carry

        lax.fori_loop(0, many // tile, settle, 0)
        for k in range(1, n):
            for index in range(per):
                push(k, index).wait_send()
            peer = lax.rem(t + k, n)
            remote(
                stats.at[t], stats.at[t], stat_send.at[k], stat_recv.at[t], at(d, sec, peer)
            ).wait_send()


def finish(n, active, gq, gkv, x, up, gain, rms, wq, wk, wv):
    many, wide = x.shape
    deep = 512
    dma = pltpu.SemaphoreType.DMA
    vmem = pl.BlockSpec(memory_space=pltpu.VMEM)
    return pl.pallas_call(
        functools.partial(finish_body, n, active, wq.shape[0]),
        in_specs=[vmem] * 6 + [pl.BlockSpec(memory_space=pl.ANY)] * 3,
        out_specs=[vmem, vmem],
        out_shape=[
            jax.ShapeDtypeStruct((many, wide), F32),
            jax.ShapeDtypeStruct((many, wide), BF16),
        ],
        scratch_shapes=[
            pltpu.VMEM((n, many, wide), BF16),
            pltpu.VMEM((n, many, wide), BF16),
            pltpu.VMEM((n, many, HD), F32),
            pltpu.VMEM((2, deep, wq.shape[1]), BF16),
            pltpu.VMEM((2, deep, wk.shape[1]), BF16),
            pltpu.VMEM((2, deep, wv.shape[1]), BF16),
            dma((2, 3)),
            dma((n, wide // deep)),
            dma((n, wide // deep)),
            dma((n,)),
            dma((n,)),
        ],
        compiler_params=pltpu.CompilerParams(
            collective_id=1 + active, has_side_effects=True, vmem_limit_bytes=BIG
        ),
    )(gq, gkv, x, up, gain, rms, wq, wk, wv)


def descend_body(
    n, g_ref, w_ref, up_out, go_out, mid, spread, w_in, outbox, inbox,
    g_send, g_recv, s_send, s_recv, p_send, p_recv, w_sem, up_sem,
):
    d, sec, t = lax.axis_index("dp"), lax.axis_index("section"), lax.axis_index("tensor")
    for k in range(n):
        greet(at(d, 1 - sec, lax.rem(t + k, n)))

    @pl.when(sec == 0)
    def _():
        for k in range(1, n):
            greet(at(lax.rem(d + k, n), sec, t))

    pl.semaphore_wait(pltpu.get_barrier_semaphore(), n + (1 - sec) * (n - 1))

    def hand(k):
        return remote(
            g_ref, mid.at[t], g_send.at[k], g_recv.at[t], at(d, 0, lax.rem(t + k, n))
        )

    @pl.when(sec == 1)
    def _():
        for k in range(n):
            hand(k).start()
        for k in range(n):
            hand(k).wait_send()

    @pl.when(sec == 0)
    def _():
        load = pltpu.make_async_copy(w_ref, w_in, w_sem)
        load.start()

        def arrived(slot):
            remote(
                mid.at[slot], mid.at[slot], g_send.at[0], g_recv.at[slot], at(d, 1, slot)
            ).wait_recv()

        onward = jnp.where(2 * t >= n, n - 1, 1)

        def move(slot):
            return remote(
                mid.at[slot], spread.at[d], s_send.at[slot], s_recv.at[d], at(slot, 0, t)
            )

        for step in range(n):
            slot = lax.rem(t + step * onward, n)
            arrived(slot)

            @pl.when(slot != d)
            def _():
                move(slot).start()

        keep = pltpu.make_async_copy(mid.at[t], up_out, up_sem)
        keep.start()
        load.wait()

        def store_own(start, size, value):
            outbox[d, :, pl.ds(start, size)] = value

        tiled_dot_t(mid.at[d], w_in, store_own)

        def give(k):
            peer = lax.rem(d + k, n)
            return remote(
                outbox.at[peer], inbox.at[d], p_send.at[k], p_recv.at[d], at(peer, 0, t)
            )

        for k in range(1, n):
            peer = lax.rem(d + k, n)
            remote(
                spread.at[peer], spread.at[peer], s_send.at[k], s_recv.at[peer],
                at(peer, 0, t),
            ).wait_recv()

            def store(start, size, value):
                outbox[peer, :, pl.ds(start, size)] = value

            tiled_dot_t(spread.at[peer], w_in, store)
            give(k).start()

        for k in range(1, n):
            peer = lax.rem(d + k, n)
            remote(
                inbox.at[peer], inbox.at[peer], p_send.at[k], p_recv.at[peer],
                at(peer, 0, t),
            ).wait_recv()
        tile = 16

        def add(index, carry):
            rows = pl.ds(pl.multiple_of(index * tile, tile), tile)
            total = outbox[d, rows, :].astype(F32)
            for k in range(1, n):
                total = total + inbox[lax.rem(d + k, n), rows, :].astype(F32)
            go_out[rows, :] = total.astype(BF16)
            return carry

        lax.fori_loop(0, go_out.shape[0] // tile, add, 0)
        keep.wait()
        for k in range(1, n):
            move(lax.rem(d + k, n)).wait_send()
            give(k).wait_send()


def descend(n, g, w):
    many, wide = g.shape
    cols = w.shape[0]
    dma = pltpu.SemaphoreType.DMA
    vmem = pl.BlockSpec(memory_space=pltpu.VMEM)
    return pl.pallas_call(
        functools.partial(descend_body, n),
        in_specs=[vmem, pl.BlockSpec(memory_space=pl.ANY)],
        out_specs=[vmem, vmem],
        out_shape=[
            jax.ShapeDtypeStruct((many, wide), BF16),
            jax.ShapeDtypeStruct((many, cols), BF16),
        ],
        scratch_shapes=[
            pltpu.VMEM((n, many, wide), BF16),
            pltpu.VMEM((n, many, wide), BF16),
            pltpu.VMEM(w.shape, BF16),
            pltpu.VMEM((n, many, cols), BF16),
            pltpu.VMEM((n, many, cols), BF16),
            dma((n,)),
            dma((n,)),
            dma((n,)),
            dma((n,)),
            dma((n,)),
            dma((n,)),
            dma,
            dma,
        ],
        compiler_params=pltpu.CompilerParams(
            collective_id=3, has_side_effects=True, vmem_limit_bytes=BIG
        ),
    )(g, w)


def attend_body(n, active, gather, lens_ref, q_ref, o_ref, kv_ref, cos_ref, sin_ref, *rest):
    if gather:
        gq_ref, gkv_ref, kv_out, kv_box, terms, inbox, kv_send, kv_recv, send, recv = rest
    else:
        gq_ref, gkv_ref, terms, inbox, send, recv = rest
        kv_box = kv_ref
    d, sec, t = lax.axis_index("dp"), lax.axis_index("section"), lax.axis_index("tensor")
    batch, rows, cols = q_ref.shape
    kv_cols = kv_box.shape[3] // 2
    kv_dev = kv_cols // HD
    group = cols // kv_cols
    length = n * rows
    many = rows * group
    scale = 1.0 / math.sqrt(HD)
    for k in range(1, n):
        greet(at(lax.rem(d + k, n), sec, t))
    pl.semaphore_wait(pltpu.get_barrier_semaphore(), n - 1)

    if gather:
        for k in range(1, n):
            remote(
                kv_ref, kv_box.at[d], kv_send.at[k], kv_recv.at[d],
                at(lax.rem(d + k, n), sec, t),
            ).start()
        kv_box[d] = kv_ref[...]
        for k in range(1, n):
            peer = lax.rem(d + k, n)
            remote(
                kv_ref, kv_box.at[peer], kv_send.at[k], kv_recv.at[peer], at(peer, sec, t)
            ).wait_recv()
        kv_out[...] = kv_box[...]

    @pl.when(sec == active)
    def _():
        cosine, sine = cos_ref[...], sin_ref[...]

        def one(index, carry):
            seq = index // kv_dev
            kv_head = lax.rem(index, kv_dev)
            k_lanes = pl.ds(pl.multiple_of(kv_head * HD, HD), HD)
            v_lanes = pl.ds(pl.multiple_of(kv_cols + kv_head * HD, HD), HD)

            def q_lanes(head):
                return pl.ds(pl.multiple_of((kv_head * group + head) * HD, HD), HD)

            q_parts, o_parts = [], []
            for head in range(group):
                raw = q_ref[seq, :, q_lanes(head)]
                turned = raw * cosine + pltpu.roll(raw, HD // 2, 1) * sine
                q_parts.append(turned.astype(BF16))
                o_parts.append(o_ref[seq, :, q_lanes(head)])
            q_all = jnp.concatenate(q_parts, 0)
            o_all = jnp.concatenate(o_parts, 0)
            keys = jnp.concatenate([kv_box[r, seq, :, k_lanes] for r in range(n)], 0)
            values = jnp.concatenate([kv_box[r, seq, :, v_lanes] for r in range(n)], 0)
            row_at = lax.broadcasted_iota(jnp.int32, (many, length), 0) & (rows - 1)
            query_at = d * rows + row_at
            key_at = lax.broadcasted_iota(jnp.int32, (many, length), 1)
            start = length - lens_ref[seq]
            allowed = (key_at == query_at) | ((key_at < query_at) & (key_at >= start))
            scores = jnp.where(allowed, dot_t(q_all, keys) * scale, -1e30)
            highest = jnp.max(scores, -1, keepdims=True)
            terms_e = jnp.where(allowed, jnp.exp(scores - highest), 0.0)
            probs = terms_e / jnp.sum(terms_e, -1, keepdims=True)
            grad_probs = dot_t(o_all, values)
            row_dot = jnp.sum(probs * grad_probs, -1, keepdims=True)
            grad_scores = (probs * (grad_probs - row_dot) * scale).astype(BF16)
            grad_qr = dot_n(grad_scores, keys)
            grad_k = dot_c(grad_scores, q_all).astype(BF16)
            grad_v = dot_c(probs.astype(BF16), o_all).astype(BF16)
            for r in range(n):
                terms[r, seq, :, k_lanes] = grad_k[r * rows : (r + 1) * rows]
                terms[r, seq, :, v_lanes] = grad_v[r * rows : (r + 1) * rows]
            for head in range(group):
                part = grad_qr[head * rows : (head + 1) * rows]
                turned = part * cosine - pltpu.roll(part, HD // 2, 1) * sine
                gq_ref[seq, :, q_lanes(head)] = turned.astype(BF16)
            return carry

        lax.fori_loop(0, batch * kv_dev, one, 0)

        def push(k):
            peer = lax.rem(d + k, n)
            return remote(
                terms.at[peer], inbox.at[d], send.at[k], recv.at[d], at(peer, sec, t)
            )

        for k in range(1, n):
            push(k).start()
        inbox[d] = terms[d]
        for k in range(1, n):
            peer = lax.rem(d + k, n)
            remote(
                terms.at[peer], inbox.at[peer], send.at[k], recv.at[peer], at(peer, sec, t)
            ).wait_recv()
        for seq in range(batch):
            total = inbox[0, seq].astype(F32)
            for r in range(1, n):
                total = total + inbox[r, seq].astype(F32)
            for head in range(kv_dev):
                lanes = slice(head * HD, (head + 1) * HD)
                part = total[:, lanes]
                turned = part * cosine - pltpu.roll(part, HD // 2, 1) * sine
                gkv_ref[seq, :, lanes] = turned.astype(BF16)
            gkv_ref[seq, :, kv_cols:] = total[:, kv_cols:].astype(BF16)
        for k in range(1, n):
            push(k).wait_send()

    if gather:
        for k in range(1, n):
            remote(
                kv_ref, kv_box.at[d], kv_send.at[k], kv_recv.at[d],
                at(lax.rem(d + k, n), sec, t),
            ).wait_send()


def attend(n, active, gather, lengths, queries, grad_out, kv, cosine, sine):
    batch, rows, cols = queries.shape
    both = kv.shape[-1]
    dma = pltpu.SemaphoreType.DMA
    vmem = pl.BlockSpec(memory_space=pltpu.VMEM)
    whole = (n, batch, rows, both)
    out_shape = [
        jax.ShapeDtypeStruct((batch, rows, cols), BF16),
        jax.ShapeDtypeStruct((batch, rows, both), BF16),
    ]
    scratch = [pltpu.VMEM(whole, BF16), pltpu.VMEM(whole, BF16)]
    sems = [dma((n,)), dma((n,))]
    if gather:
        out_shape.append(jax.ShapeDtypeStruct(whole, BF16))
        scratch.append(pltpu.VMEM(whole, BF16))
        sems = sems + sems
    return pl.pallas_call(
        functools.partial(attend_body, n, active, gather),
        in_specs=[pl.BlockSpec(memory_space=pltpu.SMEM)] + [vmem] * 5,
        out_specs=[vmem] * len(out_shape),
        out_shape=out_shape,
        scratch_shapes=scratch + sems,
        compiler_params=pltpu.CompilerParams(
            collective_id=4 + active, has_side_effects=True, vmem_limit_bytes=BIG
        ),
    )(lengths, queries, grad_out, kv, cosine, sine)


def on_device(
    n_tensor, stored, cotangent, positions, lengths, norm_gain, w_query, w_key, w_value, w_out
):
    x_own = stored[0]
    gain = norm_gain[0]
    w_q, w_k, w_v, w_o = w_query[0], w_key[0], w_value[0], w_out[0]
    seqs, rows, width_dev = x_own.shape
    many = seqs * rows
    width = gain.shape[0]
    kv_cols = w_k.shape[1]
    dp_id = lax.axis_index("dp")
    tensor_id = lax.axis_index("tensor")
    section_id = lax.axis_index("section")
    row_ids = dp_id * rows + jnp.arange(rows, dtype=jnp.int32)
    cosine, sine = angle_tables(row_ids.astype(F32))
    resp = cotangent.shape[1]
    queries, key_values, rms_wide, resp_grad = opening(
        n_tensor,
        x_own.reshape(many, width_dev),
        cotangent.reshape(seqs * resp, width_dev),
        w_o,
        gain,
        w_q,
        w_k,
        w_v,
    )
    resp_grad = resp_grad.reshape(seqs, resp, -1)
    placed = (positions[:, None, :] == row_ids[None, :, None]).astype(BF16)

    def place(small):
        return jnp.einsum("spr,srd->spd", placed, small, preferred_element_type=F32).astype(BF16)

    keys, values = key_values[:, :kv_cols], key_values[:, kv_cols:]
    k_four = keys.reshape(seqs, rows, -1, HD)
    k_rot = k_four * cosine[:, None] + turn_plain(k_four) * sine[:, None]
    kv_own = jnp.concatenate(
        [k_rot.reshape(seqs, rows, kv_cols), values.reshape(seqs, rows, kv_cols)], -1
    ).astype(BF16)
    queries = queries.reshape(seqs, rows, -1)
    gain_own = lax.dynamic_slice_in_dim(gain, tensor_id * width_dev, width_dev, 0)
    x_mine = x_own.reshape(many, width_dev)

    def backward(active, upstream_own, grad_q, grad_kv):
        return finish(
            n_tensor,
            active,
            grad_q.reshape(many, -1),
            grad_kv.reshape(many, -1),
            x_mine,
            upstream_own.reshape(many, width_dev),
            gain_own[None],
            rms_wide,
            w_q,
            w_k,
            w_v,
        )

    grad_q, grad_kv, kv_all = attend(
        n_tensor, 1, True, lengths, queries, place(resp_grad), kv_own, cosine, sine
    )
    first, first_low = backward(1, place(cotangent), grad_q, grad_kv)

    handed, grad_out = descend(n_tensor, first_low, w_o)
    grad_q, grad_kv = attend(
        n_tensor,
        0,
        False,
        lengths,
        queries,
        grad_out.reshape(seqs, rows, -1),
        kv_all,
        cosine,
        sine,
    )
    second, _ = backward(0, handed, grad_q, grad_kv)
    result = jnp.where(section_id == 0, second, first)
    return result.reshape(1, seqs, rows, width_dev)


def solution(mesh):
    return jax.shard_map(
        functools.partial(on_device, mesh.shape["tensor"]),
        mesh=mesh,
        in_specs=(
            P("section", None, "dp", "tensor"),
            P(None, None, "tensor"),
            P(),
            P(),
            P("section", None),
            P("section", None, "tensor"),
            P("section", None, "tensor"),
            P("section", None, "tensor"),
            P("section", "tensor", "dp"),
        ),
        out_specs=P("section", None, "dp", "tensor"),
        check_vma=False,
    )
```
